128 devices in a mesh: seq: 16 (over y, z), batch: 8 (over x, core).
Axes of the slice: x: 4, y: 4, z: 4, core: 2. Of those that a mesh axis runs over, the one named last changes fastest.
Arguments:
- inputs: bfloat16 [8, 16384, 2048], P('batch', 'seq'), may hold values from -6 to 6
- input_map: bfloat16 [8, 16384, 128], P('batch', 'seq'), may hold values from -0.5 to 0.5
- output_map: bfloat16 [8, 16384, 128], P('batch', 'seq'), may hold values from -0.5 to 0.5
- step_raw: float32 [8, 32, 16384], P('batch', None, 'seq'), may hold values from -4.5 to 4.5
- step_bias: float32 [32], replicated, may hold values from -2 to 0
- decay_rate: float32 [32], replicated, may hold values from 1.5258789e-05 to 0.05
- skip_gain: float32 [32], replicated, may hold values from 0.5 to 1.5
- cotangent: bfloat16 [8, 16384, 2048], P('batch', 'seq'), may hold values from -6 to 6
Outputs:
- grad_inputs: bfloat16 [8, 16384, 2048], P('batch', 'seq')
- grad_input_map: float32 [8, 16384, 128], P('batch', 'seq')
- grad_output_map: float32 [8, 16384, 128], P('batch', 'seq')
- grad_step_raw: float32 [8, 32, 16384], P('batch', None, 'seq')
- grad_params: float32 [2, 32], replicated
- grad_decay_rate: float32 [32], replicated
The draws below stay inside these ranges and needn't reach their ends.
All inputs are finite; a program needn't handle non-finite values.
Results may differ from the reference program's by a relative error of at most 0.034.
Values sent between devices are 32-bit elements; how exact they have to be, the bound alone decides.
A program may use at most 192 MiB of HBM per device.

```python
import math
import jax
import jax.numpy as jnp
from jax import lax

H = 32
P_SIZE = 64
N = 128
GROUP = 256
TOK_DEV = 1024
E = 2048
SEQLEN = 16384
SEQS = 8


def draw_step_raw(key, part):
    blocks = SEQLEN // TOK_DEV
    key_order = jax.random.fold_in(key, 11)
    key_jitter = jax.random.fold_in(key, 12)
    key_noise = jax.random.fold_in(key, 13)
    order = jax.vmap(lambda k: jax.random.permutation(k, blocks))(jax.random.split(key_order, SEQS))
    level = -2.0 + 4.0 * order.astype(jnp.float32) / max(blocks - 1, 1)
    jitter = jax.random.uniform(key_jitter, (SEQS, H, blocks), jnp.float32, -0.5, 0.5)
    offset = jnp.repeat(level[:, None, :] + jitter, TOK_DEV, axis=2)
    noise = jnp.clip(0.5 * jax.random.normal(key_noise, (SEQS, H, SEQLEN), jnp.float32), -2.0, 2.0)
    return (offset + noise).astype(jnp.float32)


def steps_of(rng, extent, cuts, least, high):
    def one(position, blocks):
        draws = jax.random.uniform(jax.random.fold_in(jax.random.fold_in(rng, 6), position), (blocks,), jnp.float32, least / len(cuts), high / len(cuts))
        return jnp.repeat(jnp.exp(draws), extent[position] // blocks).reshape((-1,) + (1,) * (len(extent) - position - 1))

    loudness = one(*cuts[0])
    for cut in cuts[1:]:
        loudness = loudness * one(*cut)
    return loudness


def normal_values(own_key, shape, spread, limit, cuts=(), kind=jnp.bfloat16):
    entries = spread * jax.random.normal(own_key, shape, jnp.float32)
    if cuts:
        entries = entries * steps_of(own_key, shape, cuts, -0.22, 0.18)
    return jnp.clip(entries, -limit, limit).astype(kind)


def setup_inputs(seed: int = 0) -> dict:
    key_list = jax.random.split(jax.random.key(seed), 9)
    return {
        "inputs": normal_values(key_list[0], (SEQS, SEQLEN, E), 1.0, 6.0, ((0, 8), (1, 16))),
        "input_map": normal_values(key_list[1], (SEQS, SEQLEN, N), N ** -0.5, 0.5, ((0, 8), (1, 16))),
        "output_map": normal_values(key_list[2], (SEQS, SEQLEN, N), N ** -0.5, 0.5, ((0, 8), (1, 16))),
        "step_raw": draw_step_raw(jax.random.fold_in(key_list[8], 71), 0),
        "step_bias": jnp.clip(jax.random.uniform(key_list[4], (H,), jnp.float32, -2.0, 0.0), -2.0, 0.0),
        "decay_rate": jnp.clip(jnp.exp(jax.random.uniform(key_list[5], (H,), jnp.float32, math.log(1.52587890625e-05), math.log(0.05))), 1.52587890625e-05, 0.05),
        "skip_gain": jnp.clip(jax.random.uniform(key_list[6], (H,), jnp.float32, 0.5, 1.5), 0.5, 1.5),
        "cotangent": normal_values(key_list[7], (SEQS, SEQLEN, E), 1.0, 6.0, ((0, 8), (1, 16))),
    }


def block_step(state, items, skip_gain):
    xc, bc, cc, stepc, logc = items
    width = xc.shape[0]
    cum = jnp.cumsum(logc, axis=1)
    rows = lax.broadcasted_iota(jnp.int32, (width, width), 0)
    cols = lax.broadcasted_iota(jnp.int32, (width, width), 1)
    lower = cols <= rows
    gap = jnp.where(lower[None], cum[:, :, None] - cum[:, None, :], -1e+30)
    decay = jnp.exp(gap)
    scores = jnp.einsum('tn,sn->ts', cc, bc, preferred_element_type=jnp.float32)
    weights = (scores[None] * decay * stepc[:, None, :]).astype(jnp.bfloat16)
    inner = jnp.einsum('hts,shp->thp', weights, xc, preferred_element_type=jnp.float32)
    carried = jnp.einsum('tn,hpn->thp', cc, state.astype(jnp.bfloat16), preferred_element_type=jnp.float32) * jnp.exp(cum).T[:, :, None]
    output = inner + carried + skip_gain[None, :, None] * xc.astype(jnp.float32)
    tail = jnp.exp(cum[:, -1:] - cum) * stepc
    scaled = (xc.astype(jnp.float32) * tail.T[:, :, None]).astype(jnp.bfloat16)
    fresh = jnp.einsum('shp,sn->hpn', scaled, bc, preferred_element_type=jnp.float32)
    new_state = jnp.exp(cum[:, -1])[:, None, None] * state + fresh
    return (new_state, output.astype(jnp.bfloat16))

def scan_forward(xb, bb, cb, raw, step_bias, decay_rate, skip_gain, start_state):
    length, heads, head_size = xb.shape
    states = bb.shape[1]
    blocks = length // GROUP
    step = jax.nn.softplus(raw + step_bias[:, None])
    logd = -decay_rate[:, None] * step
    xs = xb.reshape(blocks, GROUP, heads, head_size)
    bs = bb.reshape(blocks, GROUP, states)
    cs = cb.reshape(blocks, GROUP, states)
    steps = step.reshape(heads, blocks, GROUP).transpose(1, 0, 2)
    logs = logd.reshape(heads, blocks, GROUP).transpose(1, 0, 2)
    body_fn = jax.checkpoint(lambda s, it: block_step(s, it, skip_gain))
    end_state, outs = lax.scan(body_fn, start_state, (xs, bs, cs, steps, logs))
    return (outs.reshape(length, heads, head_size), end_state)

def reference(inputs, input_map, output_map, step_raw, step_bias, decay_rate, skip_gain, cotangent):

    def one_sequence(items):
        xs, bs, cs, raw, dys = items
        length = xs.shape[0]
        xb = xs.reshape(length, H, P_SIZE)
        dyb = dys.reshape(length, H, P_SIZE)
        zero_state = jnp.zeros((H, P_SIZE, N), jnp.float32)

        def forward(xv, bv, cv, rv, biasv, ratev, skipv):
            return scan_forward(xv, bv, cv, rv, biasv, ratev, skipv, zero_state)[0]
        outs, pull = jax.vjp(forward, xb, bs, cs, raw, step_bias, decay_rate, skip_gain)
        grads = pull(dyb)
        params = jnp.stack([grads[4], grads[5], grads[6]])
        return (grads[0].reshape(length, H * P_SIZE).astype(jnp.bfloat16), grads[1].astype(jnp.float32), grads[2].astype(jnp.float32), grads[3], params)
    gx, gb, gc, gr, gp = lax.map(one_sequence, (inputs, input_map, output_map, step_raw, cotangent))
    scale = 1.0 / math.sqrt(SEQS * SEQLEN)
    summed = lax.optimization_barrier(jnp.sum(gp, axis=0)) * scale
    return (gx, gb, gc, gr, jnp.stack([summed[0], summed[2]]), summed[1])
```

```python
import functools
import math

import jax
import jax.numpy as jnp
from jax import lax
from jax.experimental import pallas as pl
from jax.experimental.pallas import tpu as pltpu
from jax.sharding import PartitionSpec as P

GROUP = 256
LANES = 128
MESH = pl.DeviceIdType.MESH
BF = jnp.bfloat16
F32 = jnp.float32


def dot(a, b):
    return jnp.dot(a, b, preferred_element_type=F32)


def dot_nt(a, b):
    return lax.dot_general(a, b, (((1,), (1,)), ((), ())), preferred_element_type=F32)


def two_parts(v):
    high = v.astype(BF).astype(F32)
    return high, v - high


def sum_dot(v, ones):
    high, rest = two_parts(v)
    mid, low = two_parts(rest)
    rows = v.shape[0]
    out = dot(jnp.concatenate([high, mid, low], axis=0).astype(BF), ones)
    return out[:rows] + out[rows : 2 * rows] + out[2 * rows :]


def kernel(
    nseq,
    x_hbm,
    dy_hbm,
    b_ref,
    c_ref,
    raw_ref,
    par_ref,
    dx_hbm,
    db_ref,
    dc_ref,
    draw_ref,
    gpar_ref,
    x_buf,
    dy_buf,
    xt_buf,
    dyt_buf,
    fm_buf,
    dxi_buf,
    ds_buf,
    dg_buf,
    ecl_buf,
    step_buf,
    racc_buf,
    send_buf,
    recv_buf,
    back_buf,
    home_buf,
    stb_buf,
    gtb_buf,
    bdot_buf,
    ohp_buf,
    ohm_buf,
    ota_buf,
    otb_buf,
    skip_buf,
    in_sem,
    out_sem,
    s1,
    r1,
    s2,
    r2,
):
    tokens, width = x_buf.shape
    heads = raw_ref.shape[0]
    hs = width // heads
    states = b_ref.shape[1]
    blocks = tokens // GROUP
    gw = min(256, width)
    groups = width // gw
    ow = width // nseq
    me = lax.axis_index("seq")

    def rows_of(b):
        return pl.ds(b * GROUP, GROUP)

    def x_in(b):
        return pltpu.make_async_copy(x_hbm.at[rows_of(b)], x_buf.at[rows_of(b)], in_sem.at[0, b])

    def dy_in(b):
        return pltpu.make_async_copy(dy_hbm.at[rows_of(b)], dy_buf.at[rows_of(b)], in_sem.at[1, b])

    for b in range(blocks):
        x_in(b).start()
        dy_in(b).start()

    bar = pltpu.get_barrier_semaphore()
    for k in range(1, nseq):
        pl.semaphore_signal(
            bar, inc=1, device_id={"seq": lax.rem(me + k, nseq)}, device_id_type=MESH
        )

    k_id = lax.broadcasted_iota(jnp.int32, (LANES, width), 0)
    l_id = lax.broadcasted_iota(jnp.int32, (LANES, width), 1) // hs
    same = (k_id % heads) == l_id
    ohp_buf[...] = jnp.where(same & (k_id < 2 * heads), 1.0, 0.0).astype(BF)
    ohm_buf[...] = jnp.where(same & (k_id >= 2 * heads), 1.0, 0.0).astype(BF)
    j_id = lax.broadcasted_iota(jnp.int32, (width, LANES), 1)
    h_id = lax.broadcasted_iota(jnp.int32, (width, LANES), 0) // hs
    ota_buf[...] = jnp.where(j_id == h_id, 1.0, 0.0).astype(BF)
    otb_buf[...] = jnp.where(j_id == h_id + heads, 1.0, 0.0).astype(BF)

    eye = lax.broadcasted_iota(jnp.int32, (heads, LANES), 0) == lax.broadcasted_iota(
        jnp.int32, (heads, LANES), 1
    )
    head_lane = (
        lax.broadcasted_iota(jnp.int32, (heads, width), 0)
        == lax.broadcasted_iota(jnp.int32, (heads, width), 1) // hs
    )

    def column(row):
        return jnp.sum(jnp.where(eye, row, 0.0), axis=1, keepdims=True)

    def expand(col):
        return jnp.sum(jnp.where(head_lane, col, 0.0), axis=0, keepdims=True)

    def per_head(row):
        return jnp.sum(jnp.where(head_lane, row, 0.0), axis=1, keepdims=True)

    bias = column(par_ref[0:1])
    rate = column(par_ref[1:2])
    skip_row = expand(column(par_ref[2:3]))

    t_id = lax.broadcasted_iota(jnp.int32, (GROUP, GROUP), 0)
    s_id = lax.broadcasted_iota(jnp.int32, (GROUP, GROUP), 1)
    lower = s_id <= t_id
    upper = s_id >= t_id
    ones_le = jnp.where(upper, 1.0, 0.0).astype(BF)
    ones_ge = jnp.where(lower, 1.0, 0.0).astype(BF)

    skip_buf[...] = jnp.zeros_like(skip_buf)
    home_buf[...] = jnp.zeros_like(home_buf)

    def local(b, carry):
        rows = rows_of(b)
        v = raw_ref[:, pl.ds(pl.multiple_of(b * GROUP, GROUP), GROUP)] + bias
        step = jnp.maximum(v, 0.0) + jnp.log1p(jnp.exp(-jnp.abs(v)))
        step_buf[b] = step
        cum = sum_dot(-rate * step, ones_le)
        ep = jnp.exp(cum)
        em = step * jnp.exp(-cum)
        ep_hi, ep_lo = two_parts(ep)
        em_hi, em_lo = two_parts(em)
        parts = jnp.concatenate([ep_hi, ep_lo, em_hi, em_lo], axis=0).T.astype(BF)
        ecl_buf[b] = expand(ep[:, GROUP - 1 : GROUP])
        x_in(b).wait()
        dy_in(b).wait()
        bt = b_ref[rows]
        ct = c_ref[rows]

        def lane_group(g, _):
            lanes = pl.ds(pl.multiple_of(g * gw, gw), gw)
            fp = dot(parts, ohp_buf[:, lanes])
            fm = dot(parts, ohm_buf[:, lanes])
            fm_buf[rows, lanes] = fm
            xg = x_buf[rows, lanes].astype(F32)
            dyg = dy_buf[rows, lanes].astype(F32)
            xt = (xg * fm).astype(BF)
            dyt = (dyg * fp).astype(BF)
            xt_buf[rows, lanes] = xt
            dyt_buf[rows, lanes] = dyt
            prod = xg * dyg
            skip_buf[:, lanes] += jnp.sum(prod.reshape(GROUP // 8, 8, gw), axis=0)
            ds_buf[b, :, lanes] = lax.dot_general(
                bt, xt, (((0,), (0,)), ((), ())), preferred_element_type=F32
            )
            dg_buf[b, :, lanes] = lax.dot_general(
                ct, dyt, (((0,), (0,)), ((), ())), preferred_element_type=F32
            )
            return 0

        lax.fori_loop(0, groups, lane_group, 0)
        return carry

    lax.fori_loop(0, blocks, local, 0)

    for j in range(nseq):
        lanes = slice(j * ow, (j + 1) * ow)
        st = ds_buf[0, :, lanes] * ecl_buf[0, :, lanes]
        gt = dg_buf[0, :, lanes]
        decay = ecl_buf[0, :, lanes]
        for b in range(1, blocks):
            e = ecl_buf[b, :, lanes]
            st = (st + ds_buf[b, :, lanes]) * e
            gt = gt + decay * dg_buf[b, :, lanes]
            decay = decay * e
        send_buf[j, 0:states] = st
        send_buf[j, states : 2 * states] = gt
        send_buf[j, 2 * states :] = jnp.broadcast_to(decay, (8, ow))

    pl.semaphore_wait(bar, nseq - 1)

    def there(k):
        peer = lax.rem(me + k, nseq)
        return pltpu.make_async_remote_copy(
            src_ref=send_buf.at[peer],
            dst_ref=recv_buf.at[me],
            send_sem=s1.at[k],
            recv_sem=r1.at[k],
            device_id={"seq": peer},
            device_id_type=MESH,
        )

    def again(k):
        peer = lax.rem(me + k, nseq)
        return pltpu.make_async_remote_copy(
            src_ref=back_buf.at[peer],
            dst_ref=home_buf.at[me],
            send_sem=s2.at[k],
            recv_sem=r2.at[k],
            device_id={"seq": peer},
            device_id_type=MESH,
        )

    for k in range(1, nseq):
        there(k).start()
    recv_buf[me] = send_buf[me]

    def inside(b, carry):
        rows = rows_of(b)
        bt = b_ref[rows]
        ct = c_ref[rows]
        scores = jnp.where(lower, dot_nt(ct, bt), 0.0).astype(BF)
        flipped = jnp.where(upper, dot_nt(bt, ct), 0.0).astype(BF)

        def lane_group(g, acc):
            lanes = pl.ds(pl.multiple_of(g * gw, gw), gw)
            xt = xt_buf[rows, lanes]
            dyt = dyt_buf[rows, lanes]
            yi = dot(scores, xt)
            dxi = dot(flipped, dyt)
            dxi_buf[rows, lanes] = dxi
            rp = (yi * dyt.astype(F32)).astype(BF)
            cp = (dxi * xt.astype(F32)).astype(BF)
            lane_rows = pl.ds(pl.multiple_of(g * gw, gw), gw)
            racc_buf[rows] += dot(rp, ota_buf[lane_rows]) + dot(cp, otb_buf[lane_rows])
            return acc

        racc_buf[rows] = jnp.zeros((GROUP, LANES), F32)
        lax.fori_loop(0, groups, lane_group, 0)
        ds = jnp.where(lower, dot_nt(dyt_buf[rows], xt_buf[rows]), 0.0)
        dc_ref[rows] = dot(ds.astype(BF), bt)
        db_ref[rows] = dot(ds.T.astype(BF), ct)
        return carry

    lax.fori_loop(0, blocks, inside, 0)

    for k in range(1, nseq):
        there(k).wait()

    st = jnp.zeros((states, ow), F32)
    for i in range(nseq):
        back_buf[i, 0:states] = st
        st = st * recv_buf[i, 2 * states : 2 * states + 1] + recv_buf[i, 0:states]
    gt = jnp.zeros((states, ow), F32)
    for i in reversed(range(nseq)):
        back_buf[i, states : 2 * states] = gt
        gt = (
            gt * recv_buf[i, 2 * states : 2 * states + 1] + recv_buf[i, states : 2 * states]
        )

    for k in range(1, nseq):
        again(k).start()
    home_buf[me] = back_buf[me]
    for k in range(1, nseq):
        again(k).wait()

    for j in range(nseq):
        lanes = slice(j * ow, (j + 1) * ow)
        st = home_buf[j, 0:states]
        ends = []
        for b in range(blocks):
            stb_buf[b, :, lanes] = st.astype(BF)
            st = (st + ds_buf[b, :, lanes]) * ecl_buf[b, :, lanes]
            ends.append(st)
        gt = home_buf[j, states : 2 * states]
        for b in reversed(range(blocks)):
            bdot_buf[b, :, lanes] = jnp.sum(gt * ends[b], axis=0, keepdims=True)
            gt = gt * ecl_buf[b, :, lanes]
            gtb_buf[b, :, lanes] = gt.astype(BF)
            gt = gt + dg_buf[b, :, lanes]

    def dx_out(b):
        return pltpu.make_async_copy(x_buf.at[rows_of(b)], dx_hbm.at[rows_of(b)], out_sem.at[b])

    def finish(b, carry):
        gbias, grate = carry
        rows = rows_of(b)
        bt = b_ref[rows]
        ct = c_ref[rows]

        def lane_group(g, acc):
            lanes = pl.ds(pl.multiple_of(g * gw, gw), gw)
            lane_rows = pl.ds(pl.multiple_of(g * gw, gw), gw)
            yc = dot(ct, stb_buf[b, :, lanes])
            dxc = dot(bt, gtb_buf[b, :, lanes])
            rp = (yc * dyt_buf[rows, lanes].astype(F32)).astype(BF)
            cp = (dxc * xt_buf[rows, lanes].astype(F32)).astype(BF)
            racc_buf[rows] += dot(rp, ota_buf[lane_rows]) + dot(cp, otb_buf[lane_rows])
            skip = skip_row_ref[0:1, lanes]
            dx = fm_buf[rows, lanes] * (dxi_buf[rows, lanes] + dxc) + skip * dy_buf[
                rows, lanes
            ].astype(F32)
            x_buf[rows, lanes] = dx.astype(BF)
            return acc

        lax.fori_loop(0, groups, lane_group, 0)
        dx_out(b).start()
        dc_ref[rows] += dot_nt(dyt_buf[rows], stb_buf[b])
        db_ref[rows] += dot_nt(xt_buf[rows], gtb_buf[b])
        dots = racc_buf[rows].T
        rowdot = dots[0:heads]
        coldot = dots[heads : 2 * heads]
        dlog = sum_dot(rowdot - coldot, ones_ge) + per_head(bdot_buf[b])
        step = step_buf[b]
        cols = pl.ds(pl.multiple_of(b * GROUP, GROUP), GROUP)
        v = raw_ref[:, cols] + bias
        draw = (coldot / step - rate * dlog) / (1.0 + jnp.exp(-v))
        draw_ref[:, cols] = draw
        gbias = gbias + jnp.sum(draw, axis=1, keepdims=True)
        grate = grate - jnp.sum(step * dlog, axis=1, keepdims=True)
        return gbias, grate

    zero = jnp.zeros((heads, 1), F32)
    skip_row_ref = bdot_buf.at[blocks]
    skip_row_ref[...] = skip_row
    gbias, grate = lax.fori_loop(0, blocks, finish, (zero, zero))
    gskip = per_head(jnp.sum(skip_buf[...], axis=0, keepdims=True))
    lane = lax.broadcasted_iota(jnp.int32, (heads, LANES), 1)
    gpar_ref[...] = jnp.where(
        lane == 0, gbias, jnp.where(lane == 1, grate, jnp.where(lane == 2, gskip, 0.0))
    )
    for b in range(blocks):
        dx_out(b).wait()


def shards(inputs, input_map, output_map, step_raw, step_bias, decay_rate, skip_gain, cotangent):
    tokens, width = inputs.shape[1:]
    heads = step_raw.shape[1]
    states = input_map.shape[2]
    nseq = lax.axis_size("seq")
    blocks = tokens // GROUP
    ow = width // nseq
    par = jnp.pad(jnp.stack([step_bias, decay_rate, skip_gain]), ((0, 5), (0, LANES - heads)))
    vmem = pl.BlockSpec(memory_space=pltpu.VMEM)
    hbm = pl.BlockSpec(memory_space=pl.ANY)
    dma = pltpu.SemaphoreType.DMA
    dx, db, dc, draw, gpar = pl.pallas_call(
        functools.partial(kernel, nseq),
        out_shape=(
            jax.ShapeDtypeStruct((tokens, width), BF),
            jax.ShapeDtypeStruct((tokens, states), F32),
            jax.ShapeDtypeStruct((tokens, states), F32),
            jax.ShapeDtypeStruct((heads, tokens), F32),
            jax.ShapeDtypeStruct((heads, LANES), F32),
        ),
        in_specs=[hbm, hbm, vmem, vmem, vmem, vmem],
        out_specs=(hbm, vmem, vmem, vmem, vmem),
        scratch_shapes=[
            pltpu.VMEM((tokens, width), BF),
            pltpu.VMEM((tokens, width), BF),
            pltpu.VMEM((tokens, width), BF),
            pltpu.VMEM((tokens, width), BF),
            pltpu.VMEM((tokens, width), F32),
            pltpu.VMEM((tokens, width), F32),
            pltpu.VMEM((blocks, states, width), F32),
            pltpu.VMEM((blocks, states, width), F32),
            pltpu.VMEM((blocks, 1, width), F32),
            pltpu.VMEM((blocks, heads, GROUP), F32),
            pltpu.VMEM((tokens, LANES), F32),
            pltpu.VMEM((nseq, 2 * states + 8, ow), F32),
            pltpu.VMEM((nseq, 2 * states + 8, ow), F32),
            pltpu.VMEM((nseq, 2 * states, ow), F32),
            pltpu.VMEM((nseq, 2 * states, ow), F32),
            pltpu.VMEM((blocks, states, width), BF),
            pltpu.VMEM((blocks, states, width), BF),
            pltpu.VMEM((blocks + 1, 1, width), F32),
            pltpu.VMEM((LANES, width), BF),
            pltpu.VMEM((LANES, width), BF),
            pltpu.VMEM((width, LANES), BF),
            pltpu.VMEM((width, LANES), BF),
            pltpu.VMEM((8, width), F32),
            dma((2, blocks)),
            dma((blocks,)),
            dma((nseq,)),
            dma((nseq,)),
            dma((nseq,)),
            dma((nseq,)),
        ],
        compiler_params=pltpu.CompilerParams(
            collective_id=0, has_side_effects=True, vmem_limit_bytes=62 << 20
        ),
    )(inputs[0], cotangent[0], input_map[0], output_map[0], step_raw[0], par)
    total_tokens = tokens * nseq * lax.axis_size("batch")
    summed = lax.psum(gpar[:, 0:3].T, ("seq", "batch")) * (1.0 / math.sqrt(total_tokens))
    pair = jnp.stack([summed[0], summed[2]])
    return dx[None], db[None], dc[None], draw[None], pair, summed[1]


def solution(mesh):
    in_specs = (
        P("batch", "seq", None),
        P("batch", "seq", None),
        P("batch", "seq", None),
        P("batch", None, "seq"),
        P(),
        P(),
        P(),
        P("batch", "seq", None),
    )
    out_specs = (
        P("batch", "seq", None),
        P("batch", "seq", None),
        P("batch", "seq", None),
        P("batch", None, "seq"),
        P(),
        P(),
    )
    return jax.shard_map(shards, mesh=mesh, in_specs=in_specs, out_specs=out_specs, check_vma=False)
```

```python
import functools
import math

import jax
import jax.numpy as jnp
from jax import lax
from jax.experimental import pallas as pl
from jax.experimental.pallas import tpu as pltpu
from jax.sharding import PartitionSpec as P

GROUP = 256
LANES = 128
MESH = pl.DeviceIdType.MESH
BF = jnp.bfloat16
F32 = jnp.float32


def dot(a, b):
    return jnp.dot(a, b, preferred_element_type=F32)


def dot_nt(a, b):
    return lax.dot_general(a, b, (((1,), (1,)), ((), ())), preferred_element_type=F32)


def two_parts(v):
    high = v.astype(BF).astype(F32)
    return high, v - high


def sum_dot(v, ones):
    high, rest = two_parts(v)
    mid, low = two_parts(rest)
    rows = v.shape[0]
    out = dot(jnp.concatenate([high, mid, low], axis=0).astype(BF), ones)
    return out[:rows] + out[rows : 2 * rows] + out[2 * rows :]


def kernel(
    nseq,
    nbatch,
    scale,
    x_hbm,
    dy_hbm,
    b_ref,
    c_ref,
    raw_ref,
    par_ref,
    dx_hbm,
    db_ref,
    dc_ref,
    draw_ref,
    gpar_ref,
    x_buf,
    dy_buf,
    xt_buf,
    dyt_buf,
    fm_buf,
    dxi_buf,
    ds_buf,
    dg_buf,
    ecl_buf,
    step_buf,
    racc_buf,
    send_buf,
    recv_buf,
    back_buf,
    home_buf,
    stb_buf,
    gtb_buf,
    bdot_buf,
    ohp_buf,
    ohm_buf,
    ota_buf,
    otb_buf,
    skip_buf,
    in_sem,
    out_sem,
    s1,
    r1,
    s2,
    r2,
    p1_buf,
    p2_buf,
    mine_buf,
    s3,
    r3,
    s4,
    r4,
):
    tokens, width = x_buf.shape
    heads = raw_ref.shape[0]
    hs = width // heads
    states = b_ref.shape[1]
    blocks = tokens // GROUP
    gw = min(256, width)
    groups = width // gw
    ow = width // nseq
    me = lax.axis_index("seq")
    my_batch = lax.axis_index("batch")

    def rows_of(b):
        return pl.ds(b * GROUP, GROUP)

    def x_in(b):
        return pltpu.make_async_copy(x_hbm.at[rows_of(b)], x_buf.at[rows_of(b)], in_sem.at[0, b])

    def dy_in(b):
        return pltpu.make_async_copy(dy_hbm.at[rows_of(b)], dy_buf.at[rows_of(b)], in_sem.at[1, b])

    for b in range(blocks):
        x_in(b).start()
        dy_in(b).start()

    bar = pltpu.get_barrier_semaphore()
    for k in range(1, nseq):
        pl.semaphore_signal(
            bar, inc=1, device_id={"seq": lax.rem(me + k, nseq)}, device_id_type=MESH
        )
    for k in range(1, nbatch):
        pl.semaphore_signal(
            bar, inc=1, device_id={"batch": lax.rem(my_batch + k, nbatch)}, device_id_type=MESH
        )

    k_id = lax.broadcasted_iota(jnp.int32, (LANES, width), 0)
    l_id = lax.broadcasted_iota(jnp.int32, (LANES, width), 1) // hs
    same = (k_id % heads) == l_id
    ohp_buf[...] = jnp.where(same & (k_id < 2 * heads), 1.0, 0.0).astype(BF)
    ohm_buf[...] = jnp.where(same & (k_id >= 2 * heads), 1.0, 0.0).astype(BF)
    j_id = lax.broadcasted_iota(jnp.int32, (width, LANES), 1)
    h_id = lax.broadcasted_iota(jnp.int32, (width, LANES), 0) // hs
    ota_buf[...] = jnp.where(j_id == h_id, 1.0, 0.0).astype(BF)
    otb_buf[...] = jnp.where(j_id == h_id + heads, 1.0, 0.0).astype(BF)

    eye = lax.broadcasted_iota(jnp.int32, (heads, LANES), 0) == lax.broadcasted_iota(
        jnp.int32, (heads, LANES), 1
    )
    head_lane = (
        lax.broadcasted_iota(jnp.int32, (heads, width), 0)
        == lax.broadcasted_iota(jnp.int32, (heads, width), 1) // hs
    )

    def column(row):
        return jnp.sum(jnp.where(eye, row, 0.0), axis=1, keepdims=True)

    def expand(col):
        return jnp.sum(jnp.where(head_lane, col, 0.0), axis=0, keepdims=True)

    def per_head(row):
        return jnp.sum(jnp.where(head_lane, row, 0.0), axis=1, keepdims=True)

    bias = column(par_ref[0:1])
    rate = column(par_ref[1:2])
    skip_row = expand(column(par_ref[2:3]))

    t_id = lax.broadcasted_iota(jnp.int32, (GROUP, GROUP), 0)
    s_id = lax.broadcasted_iota(jnp.int32, (GROUP, GROUP), 1)
    lower = s_id <= t_id
    upper = s_id >= t_id
    ones_le = jnp.where(upper, 1.0, 0.0).astype(BF)
    ones_ge = jnp.where(lower, 1.0, 0.0).astype(BF)

    skip_buf[...] = jnp.zeros_like(skip_buf)
    home_buf[...] = jnp.zeros_like(home_buf)

    def local(b, carry):
        rows = rows_of(b)
        v = raw_ref[:, pl.ds(pl.multiple_of(b * GROUP, GROUP), GROUP)] + bias
        step = jnp.maximum(v, 0.0) + jnp.log1p(jnp.exp(-jnp.abs(v)))
        step_buf[b] = step
        cum = sum_dot(-rate * step, ones_le)
        ep = jnp.exp(cum)
        em = step * jnp.exp(-cum)
        ep_hi, ep_lo = two_parts(ep)
        em_hi, em_lo = two_parts(em)
        parts = jnp.concatenate([ep_hi, ep_lo, em_hi, em_lo], axis=0).T.astype(BF)
        ecl_buf[b] = expand(ep[:, GROUP - 1 : GROUP])
        x_in(b).wait()
        dy_in(b).wait()
        bt = b_ref[rows]
        ct = c_ref[rows]

        def lane_group(g, _):
            lanes = pl.ds(pl.multiple_of(g * gw, gw), gw)
            fp = dot(parts, ohp_buf[:, lanes])
            fm = dot(parts, ohm_buf[:, lanes])
            fm_buf[rows, lanes] = fm
            xg = x_buf[rows, lanes].astype(F32)
            dyg = dy_buf[rows, lanes].astype(F32)
            xt = (xg * fm).astype(BF)
            dyt = (dyg * fp).astype(BF)
            xt_buf[rows, lanes] = xt
            dyt_buf[rows, lanes] = dyt
            prod = xg * dyg
            skip_buf[:, lanes] += jnp.sum(prod.reshape(GROUP // 8, 8, gw), axis=0)
            ds_buf[b, :, lanes] = lax.dot_general(
                bt, xt, (((0,), (0,)), ((), ())), preferred_element_type=F32
            )
            dg_buf[b, :, lanes] = lax.dot_general(
                ct, dyt, (((0,), (0,)), ((), ())), preferred_element_type=F32
            )
            return 0

        lax.fori_loop(0, groups, lane_group, 0)
        return carry

    lax.fori_loop(0, blocks, local, 0)

    for j in range(nseq):
        lanes = slice(j * ow, (j + 1) * ow)
        st = ds_buf[0, :, lanes] * ecl_buf[0, :, lanes]
        gt = dg_buf[0, :, lanes]
        decay = ecl_buf[0, :, lanes]
        for b in range(1, blocks):
            e = ecl_buf[b, :, lanes]
            st = (st + ds_buf[b, :, lanes]) * e
            gt = gt + decay * dg_buf[b, :, lanes]
            decay = decay * e
        send_buf[j, 0:states] = st
        send_buf[j, states : 2 * states] = gt
        send_buf[j, 2 * states :] = jnp.broadcast_to(decay, (8, ow))

    pl.semaphore_wait(bar, nseq + nbatch - 2)

    def there(k):
        peer = lax.rem(me + k, nseq)
        return pltpu.make_async_remote_copy(
            src_ref=send_buf.at[peer],
            dst_ref=recv_buf.at[me],
            send_sem=s1.at[k],
            recv_sem=r1.at[k],
            device_id={"seq": peer},
            device_id_type=MESH,
        )

    def again(k):
        peer = lax.rem(me + k, nseq)
        return pltpu.make_async_remote_copy(
            src_ref=back_buf.at[peer],
            dst_ref=home_buf.at[me],
            send_sem=s2.at[k],
            recv_sem=r2.at[k],
            device_id={"seq": peer},
            device_id_type=MESH,
        )

    for k in range(1, nseq):
        there(k).start()
    recv_buf[me] = send_buf[me]

    def inside(b, carry):
        rows = rows_of(b)
        bt = b_ref[rows]
        ct = c_ref[rows]
        scores = jnp.where(lower, dot_nt(ct, bt), 0.0).astype(BF)
        flipped = jnp.where(upper, dot_nt(bt, ct), 0.0).astype(BF)

        def lane_group(g, acc):
            lanes = pl.ds(pl.multiple_of(g * gw, gw), gw)
            xt = xt_buf[rows, lanes]
            dyt = dyt_buf[rows, lanes]
            yi = dot(scores, xt)
            dxi = dot(flipped, dyt)
            dxi_buf[rows, lanes] = dxi
            rp = (yi * dyt.astype(F32)).astype(BF)
            cp = (dxi * xt.astype(F32)).astype(BF)
            lane_rows = pl.ds(pl.multiple_of(g * gw, gw), gw)
            racc_buf[rows] += dot(rp, ota_buf[lane_rows]) + dot(cp, otb_buf[lane_rows])
            return acc

        racc_buf[rows] = jnp.zeros((GROUP, LANES), F32)
        lax.fori_loop(0, groups, lane_group, 0)
        ds = jnp.where(lower, dot_nt(dyt_buf[rows], xt_buf[rows]), 0.0)
        dc_ref[rows] = dot(ds.astype(BF), bt)
        db_ref[rows] = dot(ds.T.astype(BF), ct)
        return carry

    lax.fori_loop(0, blocks, inside, 0)

    for k in range(1, nseq):
        there(k).wait()

    st = jnp.zeros((states, ow), F32)
    for i in range(nseq):
        back_buf[i, 0:states] = st
        st = st * recv_buf[i, 2 * states : 2 * states + 1] + recv_buf[i, 0:states]
    gt = jnp.zeros((states, ow), F32)
    for i in reversed(range(nseq)):
        back_buf[i, states : 2 * states] = gt
        gt = (
            gt * recv_buf[i, 2 * states : 2 * states + 1] + recv_buf[i, states : 2 * states]
        )

    for k in range(1, nseq):
        again(k).start()
    home_buf[me] = back_buf[me]
    for k in range(1, nseq):
        again(k).wait()

    for j in range(nseq):
        lanes = slice(j * ow, (j + 1) * ow)
        st = home_buf[j, 0:states]
        ends = []
        for b in range(blocks):
            stb_buf[b, :, lanes] = st.astype(BF)
            st = (st + ds_buf[b, :, lanes]) * ecl_buf[b, :, lanes]
            ends.append(st)
        gt = home_buf[j, states : 2 * states]
        for b in reversed(range(blocks)):
            bdot_buf[b, :, lanes] = jnp.sum(gt * ends[b], axis=0, keepdims=True)
            gt = gt * ecl_buf[b, :, lanes]
            gtb_buf[b, :, lanes] = gt.astype(BF)
            gt = gt + dg_buf[b, :, lanes]

    def dx_out(b):
        return pltpu.make_async_copy(x_buf.at[rows_of(b)], dx_hbm.at[rows_of(b)], out_sem.at[b])

    def finish(b, carry):
        gbias, grate = carry
        rows = rows_of(b)
        bt = b_ref[rows]
        ct = c_ref[rows]

        def lane_group(g, acc):
            lanes = pl.ds(pl.multiple_of(g * gw, gw), gw)
            lane_rows = pl.ds(pl.multiple_of(g * gw, gw), gw)
            yc = dot(ct, stb_buf[b, :, lanes])
            dxc = dot(bt, gtb_buf[b, :, lanes])
            rp = (yc * dyt_buf[rows, lanes].astype(F32)).astype(BF)
            cp = (dxc * xt_buf[rows, lanes].astype(F32)).astype(BF)
            racc_buf[rows] += dot(rp, ota_buf[lane_rows]) + dot(cp, otb_buf[lane_rows])
            skip = skip_row_ref[0:1, lanes]
            dx = fm_buf[rows, lanes] * (dxi_buf[rows, lanes] + dxc) + skip * dy_buf[
                rows, lanes
            ].astype(F32)
            x_buf[rows, lanes] = dx.astype(BF)
            return acc

        lax.fori_loop(0, groups, lane_group, 0)
        dx_out(b).start()
        dc_ref[rows] += dot_nt(dyt_buf[rows], stb_buf[b])
        db_ref[rows] += dot_nt(xt_buf[rows], gtb_buf[b])
        dots = racc_buf[rows].T
        rowdot = dots[0:heads]
        coldot = dots[heads : 2 * heads]
        dlog = sum_dot(rowdot - coldot, ones_ge) + per_head(bdot_buf[b])
        step = step_buf[b]
        cols = pl.ds(pl.multiple_of(b * GROUP, GROUP), GROUP)
        v = raw_ref[:, cols] + bias
        draw = (coldot / step - rate * dlog) / (1.0 + jnp.exp(-v))
        draw_ref[:, cols] = draw
        gbias = gbias + jnp.sum(draw, axis=1, keepdims=True)
        grate = grate - jnp.sum(step * dlog, axis=1, keepdims=True)
        return gbias, grate

    zero = jnp.zeros((heads, 1), F32)
    skip_row_ref = bdot_buf.at[blocks]
    skip_row_ref[...] = skip_row
    gbias, grate = lax.fori_loop(0, blocks, finish, (zero, zero))
    gskip = per_head(jnp.sum(skip_buf[...], axis=0, keepdims=True))

    def row(col):
        return jnp.sum(jnp.where(eye, col, 0.0), axis=0, keepdims=True)

    mine_buf[0] = jnp.concatenate(
        [row(gbias), row(gskip), row(grate), jnp.zeros((5, LANES), F32)], axis=0
    )

    def over_seq(k):
        peer = lax.rem(me + k, nseq)
        return pltpu.make_async_remote_copy(
            src_ref=mine_buf.at[0],
            dst_ref=p1_buf.at[me],
            send_sem=s3.at[k],
            recv_sem=r3.at[k],
            device_id={"seq": peer},
            device_id_type=MESH,
        )

    def over_batch(k):
        peer = lax.rem(my_batch + k, nbatch)
        return pltpu.make_async_remote_copy(
            src_ref=mine_buf.at[1],
            dst_ref=p2_buf.at[my_batch],
            send_sem=s4.at[k],
            recv_sem=r4.at[k],
            device_id={"batch": peer},
            device_id_type=MESH,
        )

    for k in range(1, nseq):
        over_seq(k).start()
    p1_buf[me] = mine_buf[0]
    for k in range(1, nseq):
        over_seq(k).wait()
    total = p1_buf[0]
    for i in range(1, nseq):
        total = total + p1_buf[i]
    mine_buf[1] = total
    for k in range(1, nbatch):
        over_batch(k).start()
    p2_buf[my_batch] = total
    for k in range(1, nbatch):
        over_batch(k).wait()
    total = p2_buf[0]
    for i in range(1, nbatch):
        total = total + p2_buf[i]
    gpar_ref[...] = total * scale
    for b in range(blocks):
        dx_out(b).wait()


def shards(inputs, input_map, output_map, step_raw, step_bias, decay_rate, skip_gain, cotangent):
    tokens, width = inputs.shape[1:]
    heads = step_raw.shape[1]
    states = input_map.shape[2]
    nseq = lax.axis_size("seq")
    nbatch = lax.axis_size("batch")
    blocks = tokens // GROUP
    ow = width // nseq
    par = jnp.pad(jnp.stack([step_bias, decay_rate, skip_gain]), ((0, 5), (0, LANES - heads)))
    vmem = pl.BlockSpec(memory_space=pltpu.VMEM)
    hbm = pl.BlockSpec(memory_space=pl.ANY)
    dma = pltpu.SemaphoreType.DMA
    dx, db, dc, draw, gpar = pl.pallas_call(
        functools.partial(kernel, nseq, nbatch, 1.0 / math.sqrt(tokens * nseq * nbatch)),
        out_shape=(
            jax.ShapeDtypeStruct((tokens, width), BF),
            jax.ShapeDtypeStruct((tokens, states), F32),
            jax.ShapeDtypeStruct((tokens, states), F32),
            jax.ShapeDtypeStruct((heads, tokens), F32),
            jax.ShapeDtypeStruct((8, LANES), F32),
        ),
        in_specs=[hbm, hbm, vmem, vmem, vmem, vmem],
        out_specs=(hbm, vmem, vmem, vmem, vmem),
        scratch_shapes=[
            pltpu.VMEM((tokens, width), BF),
            pltpu.VMEM((tokens, width), BF),
            pltpu.VMEM((tokens, width), BF),
            pltpu.VMEM((tokens, width), BF),
            pltpu.VMEM((tokens, width), F32),
            pltpu.VMEM((tokens, width), F32),
            pltpu.VMEM((blocks, states, width), F32),
            pltpu.VMEM((blocks, states, width), F32),
            pltpu.VMEM((blocks, 1, width), F32),
            pltpu.VMEM((blocks, heads, GROUP), F32),
            pltpu.VMEM((tokens, LANES), F32),
            pltpu.VMEM((nseq, 2 * states + 8, ow), F32),
            pltpu.VMEM((nseq, 2 * states + 8, ow), F32),
            pltpu.VMEM((nseq, 2 * states, ow), F32),
            pltpu.VMEM((nseq, 2 * states, ow), F32),
            pltpu.VMEM((blocks, states, width), BF),
            pltpu.VMEM((blocks, states, width), BF),
            pltpu.VMEM((blocks + 1, 1, width), F32),
            pltpu.VMEM((LANES, width), BF),
            pltpu.VMEM((LANES, width), BF),
            pltpu.VMEM((width, LANES), BF),
            pltpu.VMEM((width, LANES), BF),
            pltpu.VMEM((8, width), F32),
            dma((2, blocks)),
            dma((blocks,)),
            dma((nseq,)),
            dma((nseq,)),
            dma((nseq,)),
            dma((nseq,)),
            pltpu.VMEM((nseq, 8, LANES), F32),
            pltpu.VMEM((nbatch, 8, LANES), F32),
            pltpu.VMEM((2, 8, LANES), F32),
            dma((nseq,)),
            dma((nseq,)),
            dma((nbatch,)),
            dma((nbatch,)),
        ],
        compiler_params=pltpu.CompilerParams(
            collective_id=0, has_side_effects=True, vmem_limit_bytes=62 << 20
        ),
    )(inputs[0], cotangent[0], input_map[0], output_map[0], step_raw[0], par)
    return dx[None], db[None], dc[None], draw[None], gpar[0:2, 0:heads], gpar[2, 0:heads]


def solution(mesh):
    in_specs = (
        P("batch", "seq", None),
        P("batch", "seq", None),
        P("batch", "seq", None),
        P("batch", None, "seq"),
        P(),
        P(),
        P(),
        P("batch", "seq", None),
    )
    out_specs = (
        P("batch", "seq", None),
        P("batch", "seq", None),
        P("batch", "seq", None),
        P("batch", None, "seq"),
        P(),
        P(),
    )
    return jax.shard_map(shards, mesh=mesh, in_specs=in_specs, out_specs=out_specs, check_vma=False)
```

```python
import functools
import math

import jax
import jax.numpy as jnp
from jax import lax
from jax.experimental import pallas as pl
from jax.experimental.pallas import tpu as pltpu
from jax.sharding import PartitionSpec as P

GROUP = 256
LANES = 128
PARTS = 4
MESH = pl.DeviceIdType.MESH
BF = jnp.bfloat16
F32 = jnp.float32


def dot(a, b):
    return jnp.dot(a, b, preferred_element_type=F32)


def dot_nt(a, b):
    return lax.dot_general(a, b, (((1,), (1,)), ((), ())), preferred_element_type=F32)


def two_parts(v):
    high = v.astype(BF).astype(F32)
    return high, v - high


def sum_dot(v, ones):
    high, rest = two_parts(v)
    mid, low = two_parts(rest)
    rows = v.shape[0]
    out = dot(jnp.concatenate([high, mid, low], axis=0).astype(BF), ones)
    return out[:rows] + out[rows : 2 * rows] + out[2 * rows :]


def kernel(
    nseq,
    nbatch,
    parts,
    scale,
    x_hbm,
    dy_hbm,
    b_ref,
    c_ref,
    raw_ref,
    par_ref,
    dx_hbm,
    db_ref,
    dc_ref,
    draw_ref,
    gpar_ref,
    x_buf,
    dy_buf,
    dyt_buf,
    fm_buf,
    dxp_buf,
    ds_buf,
    dg_buf,
    ecl_buf,
    step_buf,
    fac_buf,
    bt_buf,
    ct_buf,
    low_buf,
    up_buf,
    dsm_buf,
    rc_buf,
    racc_buf,
    send_buf,
    recv_buf,
    back_buf,
    home_buf,
    stb_buf,
    gtb_buf,
    bdot_buf,
    ohp_buf,
    ohm_buf,
    ot_buf,
    skip_buf,
    skiprow_buf,
    dec_buf,
    decs_buf,
    decx_buf,
    p1_buf,
    p2_buf,
    mine_buf,
    in_sem,
    out_sem,
    s0,
    r0,
    s1,
    r1,
    s2,
    r2,
    s3,
    r3,
    s4,
    r4,
):
    tokens, width = x_buf.shape
    heads = raw_ref.shape[0]
    hs = width // heads
    states = b_ref.shape[1]
    blocks = tokens // GROUP
    pw = width // parts
    gw = min(256, pw)
    groups = pw // gw
    rn = states // nseq
    chunk = max(rn, 16)
    me = lax.axis_index("seq")
    my_batch = lax.axis_index("batch")

    def rows_of(b):
        return pl.ds(pl.multiple_of(b * GROUP, GROUP), GROUP)

    def x_in(b):
        return pltpu.make_async_copy(x_hbm.at[rows_of(b)], x_buf.at[rows_of(b)], in_sem.at[0, b])

    def dy_in(b):
        return pltpu.make_async_copy(dy_hbm.at[rows_of(b)], dy_buf.at[rows_of(b)], in_sem.at[1, b])

    for b in range(blocks):
        x_in(b).start()
        dy_in(b).start()

    bar = pltpu.get_barrier_semaphore()
    for k in range(1, nseq):
        pl.semaphore_signal(
            bar, inc=1, device_id={"seq": lax.rem(me + k, nseq)}, device_id_type=MESH
        )
    for k in range(1, nbatch):
        pl.semaphore_signal(
            bar, inc=1, device_id={"batch": lax.rem(my_batch + k, nbatch)}, device_id_type=MESH
        )

    k_id = lax.broadcasted_iota(jnp.int32, (LANES, width), 0)
    l_id = lax.broadcasted_iota(jnp.int32, (LANES, width), 1) // hs
    same = (k_id % heads) == l_id
    ohp_buf[...] = jnp.where(same & (k_id < 2 * heads), 1.0, 0.0).astype(BF)
    ohm_buf[...] = jnp.where(same & (k_id >= 2 * heads), 1.0, 0.0).astype(BF)
    j_id = lax.broadcasted_iota(jnp.int32, (pw, LANES), 1)
    h_id = lax.broadcasted_iota(jnp.int32, (pw, LANES), 0) // hs
    for q in range(parts):
        h_q = h_id + q * (pw // hs)
        ot_buf[q, 0:pw] = jnp.where(j_id == h_q, 1.0, 0.0).astype(BF)
        ot_buf[q, pw:] = jnp.where(j_id == h_q + heads, 1.0, 0.0).astype(BF)

    eye = lax.broadcasted_iota(jnp.int32, (heads, LANES), 0) == lax.broadcasted_iota(
        jnp.int32, (heads, LANES), 1
    )
    head_lane = (
        lax.broadcasted_iota(jnp.int32, (heads, width), 0)
        == lax.broadcasted_iota(jnp.int32, (heads, width), 1) // hs
    )

    def column(row):
        return jnp.sum(jnp.where(eye, row, 0.0), axis=1, keepdims=True)

    def row(col):
        return jnp.sum(jnp.where(eye, col, 0.0), axis=0, keepdims=True)

    def expand(col):
        return jnp.sum(jnp.where(head_lane, col, 0.0), axis=0, keepdims=True)

    def per_head(line):
        return jnp.sum(jnp.where(head_lane, line, 0.0), axis=1, keepdims=True)

    bias = column(par_ref[0:1])
    rate = column(par_ref[1:2])
    skiprow_buf[...] = expand(column(par_ref[2:3]))

    t_id = lax.broadcasted_iota(jnp.int32, (GROUP, GROUP), 0)
    s_id = lax.broadcasted_iota(jnp.int32, (GROUP, GROUP), 1)
    lower = s_id <= t_id
    upper = s_id >= t_id
    ones_le = jnp.where(upper, 1.0, 0.0).astype(BF)
    ones_ge = jnp.where(lower, 1.0, 0.0).astype(BF)

    skip_buf[...] = jnp.zeros_like(skip_buf)
    home_buf[...] = jnp.zeros_like(home_buf)

    def factors(b, total):
        v = raw_ref[:, rows_of(b)] + bias
        step = jnp.maximum(v, 0.0) + jnp.log1p(jnp.exp(-jnp.abs(v)))
        step_buf[b] = step
        cum = sum_dot(-rate * step, ones_le)
        ep = jnp.exp(cum)
        em = step * jnp.exp(-cum)
        ep_hi, ep_lo = two_parts(ep)
        em_hi, em_lo = two_parts(em)
        fac_buf[b] = jnp.concatenate([ep_hi, ep_lo, em_hi, em_lo], axis=0).T.astype(BF)
        ecl_buf[b] = expand(ep[:, GROUP - 1 : GROUP])
        bt_buf[b] = b_ref[rows_of(b)].astype(F32).T.astype(BF)
        ct_buf[b] = c_ref[rows_of(b)].astype(F32).T.astype(BF)
        return total * ep[:, GROUP - 1 : GROUP]

    total = lax.fori_loop(0, blocks, factors, jnp.ones((heads, 1), F32))
    dec_buf[...] = jnp.broadcast_to(row(total), (8, LANES))

    def local(q):
        def one_block(b, carry):
            rows = rows_of(b)
            if q == 0:
                x_in(b).wait()
                dy_in(b).wait()
            fac = fac_buf[b]
            bt = bt_buf[b]
            ct = ct_buf[b]
            for g in range(groups):
                lanes = slice(q * pw + g * gw, q * pw + (g + 1) * gw)
                fp = dot(fac, ohp_buf[:, lanes])
                fm = dot(fac, ohm_buf[:, lanes])
                fm_buf[rows, lanes] = fm
                xg = x_buf[rows, lanes].astype(F32)
                dyg = dy_buf[rows, lanes].astype(F32)
                xt = (xg * fm).astype(BF)
                dyt = (dyg * fp).astype(BF)
                x_buf[rows, lanes] = xt
                dyt_buf[rows, lanes] = dyt
                prod = xg * dyg
                skip_buf[:, lanes] += jnp.sum(prod.reshape(GROUP // 8, 8, gw), axis=0)
                ds_buf[b, :, lanes] = dot(bt, xt)
                dg_buf[b, :, lanes] = dot(ct, dyt)
            return carry

        lax.fori_loop(0, blocks, one_block, 0)
        lanes = slice(q * pw, (q + 1) * pw)
        for j in range(nseq):
            n = slice(j * rn, (j + 1) * rn)
            st = ds_buf[0, n, lanes] * ecl_buf[0, :, lanes]
            gt = dg_buf[0, n, lanes]
            decay = ecl_buf[0, :, lanes]
            for b in range(1, blocks):
                e = ecl_buf[b, :, lanes]
                st = (st + ds_buf[b, n, lanes]) * e
                gt = gt + decay * dg_buf[b, n, lanes]
                decay = decay * e
            send_buf[q, j, 0:rn] = st
            send_buf[q, j, rn:] = gt

    def decays(k):
        peer = lax.rem(me + k, nseq)
        return pltpu.make_async_remote_copy(
            src_ref=dec_buf,
            dst_ref=decs_buf.at[me],
            send_sem=s0.at[k],
            recv_sem=r0.at[k],
            device_id={"seq": peer},
            device_id_type=MESH,
        )

    def there(q, k):
        peer = lax.rem(me + k, nseq)
        return pltpu.make_async_remote_copy(
            src_ref=send_buf.at[q, peer],
            dst_ref=recv_buf.at[q, me],
            send_sem=s1.at[q, k],
            recv_sem=r1.at[q, k],
            device_id={"seq": peer},
            device_id_type=MESH,
        )

    def again(q, k):
        peer = lax.rem(me + k, nseq)
        return pltpu.make_async_remote_copy(
            src_ref=back_buf.at[q, peer],
            dst_ref=home_buf.at[q, me],
            send_sem=s2.at[q, k],
            recv_sem=r2.at[q, k],
            device_id={"seq": peer},
            device_id_type=MESH,
        )

    def scores(b, carry):
        bb = b_ref[rows_of(b)]
        cc = c_ref[rows_of(b)]
        low_buf[b] = jnp.where(lower, dot_nt(cc, bb), 0.0).astype(BF)
        up_buf[b] = jnp.where(upper, dot_nt(bb, cc), 0.0).astype(BF)
        return carry

    def inside(q):
        def one_block(b, carry):
            rows = rows_of(b)
            low = low_buf[b]
            up = up_buf[b]
            for g in range(groups):
                lanes = slice(q * pw + g * gw, q * pw + (g + 1) * gw)
                xt = x_buf[rows, lanes]
                dyt = dyt_buf[rows, lanes]
                yi = dot(low, xt)
                dxi = dot(up, dyt)
                rc_buf[:, g * gw : (g + 1) * gw] = (yi * dyt.astype(F32)).astype(BF)
                rc_buf[:, pw + g * gw : pw + (g + 1) * gw] = (dxi * xt.astype(F32)).astype(BF)
                dxp_buf[rows, lanes] = fm_buf[rows, lanes] * dxi + skiprow_buf[
                    :, lanes
                ] * dy_buf[rows, lanes].astype(F32)
            red = dot(rc_buf[...], ot_buf[q])
            lanes = slice(q * pw, (q + 1) * pw)
            ds = dot_nt(dyt_buf[rows, lanes], x_buf[rows, lanes])
            if q > 0:
                red = red + racc_buf[rows]
                ds = ds + dsm_buf[b]
            racc_buf[rows] = red
            if q < parts - 1:
                dsm_buf[b] = ds
            else:
                ds = jnp.where(lower, ds, 0.0)
                dc_ref[rows] = dot(ds.astype(BF), b_ref[rows])
                db_ref[rows] = dot(ds.T.astype(BF), c_ref[rows])
            return carry

        lax.fori_loop(0, blocks, one_block, 0)

    def scan(q):
        lanes = slice(q * pw, (q + 1) * pw)
        for k in range(1, nseq):
            there(q, k).wait()
        st = jnp.zeros((rn, pw), F32)
        gt = jnp.zeros((rn, pw), F32)
        for i in range(nseq):
            back_buf[q, i, 0:rn] = st
            st = st * decx_buf[i : i + 1, lanes] + recv_buf[q, i, 0:rn]
            h = nseq - 1 - i
            back_buf[q, h, rn:] = gt
            gt = gt * decx_buf[h : h + 1, lanes] + recv_buf[q, h, rn:]
        for k in range(1, nseq):
            again(q, k).start()
        home_buf[q, me] = back_buf[q, me]

    def entering(q):
        lanes = slice(q * pw, (q + 1) * pw)
        for k in range(1, nseq):
            again(q, k).wait()
        dots = [jnp.zeros((8, pw), F32) for _ in range(blocks)]
        for i in range(states // chunk):
            n = slice(i * chunk, (i + 1) * chunk)
            js = range(i * chunk // rn, (i + 1) * chunk // rn)
            st = jnp.concatenate([home_buf[q, j, 0:rn] for j in js], axis=0)
            ends = []
            for b in range(blocks):
                stb_buf[b, n, lanes] = st.astype(BF)
                st = (st + ds_buf[b, n, lanes]) * ecl_buf[b, :, lanes]
                ends.append(st)
            gt = jnp.concatenate([home_buf[q, j, rn:] for j in js], axis=0)
            for b in reversed(range(blocks)):
                prod = gt * ends[b]
                dots[b] = dots[b] + jnp.sum(prod.reshape(chunk // 8, 8, pw), axis=0)
                gt = gt * ecl_buf[b, :, lanes]
                gtb_buf[b, n, lanes] = gt.astype(BF)
                gt = gt + dg_buf[b, n, lanes]
        for b in range(blocks):
            bdot_buf[b, :, lanes] = dots[b]

    def dx_out(q, b):
        lanes = slice(q * pw, (q + 1) * pw)
        return pltpu.make_async_copy(
            dy_buf.at[rows_of(b), lanes], dx_hbm.at[rows_of(b), lanes], out_sem.at[q, b]
        )

    def finish(q):
        def one_block(b, carry):
            rows = rows_of(b)
            bb = b_ref[rows]
            cc = c_ref[rows]
            for g in range(groups):
                lanes = slice(q * pw + g * gw, q * pw + (g + 1) * gw)
                yc = dot(cc, stb_buf[b, :, lanes])
                dxc = dot(bb, gtb_buf[b, :, lanes])
                rc_buf[:, g * gw : (g + 1) * gw] = (
                    yc * dyt_buf[rows, lanes].astype(F32)
                ).astype(BF)
                rc_buf[:, pw + g * gw : pw + (g + 1) * gw] = (
                    dxc * x_buf[rows, lanes].astype(F32)
                ).astype(BF)
                dx = fm_buf[rows, lanes] * dxc + dxp_buf[rows, lanes]
                dy_buf[rows, lanes] = dx.astype(BF)
            dx_out(q, b).start()
            lanes = slice(q * pw, (q + 1) * pw)
            red = racc_buf[rows] + dot(rc_buf[...], ot_buf[q])
            dc_ref[rows] += dot_nt(dyt_buf[rows, lanes], stb_buf[b, :, lanes])
            db_ref[rows] += dot_nt(x_buf[rows, lanes], gtb_buf[b, :, lanes])
            if q < parts - 1:
                racc_buf[rows] = red
                return carry
            gbias, grate = carry
            dots = red.T
            rowdot = dots[0:heads]
            coldot = dots[heads : 2 * heads]
            ends = per_head(jnp.sum(bdot_buf[b], axis=0, keepdims=True))
            dlog = sum_dot(rowdot - coldot, ones_ge) + ends
            step = step_buf[b]
            v = raw_ref[:, rows] + bias
            draw = (coldot / step - rate * dlog) / (1.0 + jnp.exp(-v))
            draw_ref[:, rows] = draw
            gbias = gbias + jnp.sum(draw, axis=1, keepdims=True)
            grate = grate - jnp.sum(step * dlog, axis=1, keepdims=True)
            return gbias, grate

        zero = jnp.zeros((heads, 1), F32)
        return lax.fori_loop(0, blocks, one_block, (zero, zero))

    for q in range(parts):
        local(q)
        if q == 0:
            pl.semaphore_wait(bar, nseq + nbatch - 2)
            for k in range(1, nseq):
                decays(k).start()
            decs_buf[me] = dec_buf[...]
        for k in range(1, nseq):
            there(q, k).start()
        recv_buf[q, me] = send_buf[q, me]

    lax.fori_loop(0, blocks, scores, 0)
    for q in range(parts):
        inside(q)
        if q == 0:
            for k in range(1, nseq):
                decays(k).wait()
            every = jnp.concatenate([decs_buf[i, 0:1] for i in range(nseq)], axis=0)
            high, rest = two_parts(every)
            mid, low = two_parts(rest)
            decx_buf[...] = (
                dot(high.astype(BF), ohp_buf[...])
                + dot(mid.astype(BF), ohp_buf[...])
                + dot(low.astype(BF), ohp_buf[...])
            )
        scan(q)

    for q in range(parts):
        entering(q)
        gbias, grate = finish(q)
    gskip = per_head(jnp.sum(skip_buf[...], axis=0, keepdims=True))

    mine_buf[0] = jnp.concatenate(
        [row(gbias), row(gskip), row(grate), jnp.zeros((5, LANES), F32)], axis=0
    )

    def over_seq(k):
        peer = lax.rem(me + k, nseq)
        return pltpu.make_async_remote_copy(
            src_ref=mine_buf.at[0],
            dst_ref=p1_buf.at[me],
            send_sem=s3.at[k],
            recv_sem=r3.at[k],
            device_id={"seq": peer},
            device_id_type=MESH,
        )

    def over_batch(k):
        peer = lax.rem(my_batch + k, nbatch)
        return pltpu.make_async_remote_copy(
            src_ref=mine_buf.at[1],
            dst_ref=p2_buf.at[my_batch],
            send_sem=s4.at[k],
            recv_sem=r4.at[k],
            device_id={"batch": peer},
            device_id_type=MESH,
        )

    for k in range(1, nseq):
        over_seq(k).start()
    p1_buf[me] = mine_buf[0]
    for k in range(1, nseq):
        over_seq(k).wait()
    total = p1_buf[0]
    for i in range(1, nseq):
        total = total + p1_buf[i]
    mine_buf[1] = total
    for k in range(1, nbatch):
        over_batch(k).start()
    p2_buf[my_batch] = total
    for k in range(1, nbatch):
        over_batch(k).wait()
    total = p2_buf[0]
    for i in range(1, nbatch):
        total = total + p2_buf[i]
    gpar_ref[...] = total * scale
    for b in range(blocks):
        for q in range(parts):
            dx_out(q, b).wait()


def shards(inputs, input_map, output_map, step_raw, step_bias, decay_rate, skip_gain, cotangent):
    tokens, width = inputs.shape[1:]
    heads = step_raw.shape[1]
    states = input_map.shape[2]
    nseq = lax.axis_size("seq")
    nbatch = lax.axis_size("batch")
    blocks = tokens // GROUP
    pw = width // PARTS
    rn = states // nseq
    par = jnp.pad(jnp.stack([step_bias, decay_rate, skip_gain]), ((0, 5), (0, LANES - heads)))
    vmem = pl.BlockSpec(memory_space=pltpu.VMEM)
    hbm = pl.BlockSpec(memory_space=pl.ANY)
    dma = pltpu.SemaphoreType.DMA
    dx, db, dc, draw, gpar = pl.pallas_call(
        functools.partial(kernel, nseq, nbatch, PARTS, 1.0 / math.sqrt(tokens * nseq * nbatch)),
        out_shape=(
            jax.ShapeDtypeStruct((tokens, width), BF),
            jax.ShapeDtypeStruct((tokens, states), F32),
            jax.ShapeDtypeStruct((tokens, states), F32),
            jax.ShapeDtypeStruct((heads, tokens), F32),
            jax.ShapeDtypeStruct((8, LANES), F32),
        ),
        in_specs=[hbm, hbm, vmem, vmem, vmem, vmem],
        out_specs=(hbm, vmem, vmem, vmem, vmem),
        scratch_shapes=[
            pltpu.VMEM((tokens, width), BF),
            pltpu.VMEM((tokens, width), BF),
            pltpu.VMEM((tokens, width), BF),
            pltpu.VMEM((tokens, width), F32),
            pltpu.VMEM((tokens, width), F32),
            pltpu.VMEM((blocks, states, width), F32),
            pltpu.VMEM((blocks, states, width), F32),
            pltpu.VMEM((blocks, 1, width), F32),
            pltpu.VMEM((blocks, heads, GROUP), F32),
            pltpu.VMEM((blocks, GROUP, LANES), BF),
            pltpu.VMEM((blocks, states, GROUP), BF),
            pltpu.VMEM((blocks, states, GROUP), BF),
            pltpu.VMEM((blocks, GROUP, GROUP), BF),
            pltpu.VMEM((blocks, GROUP, GROUP), BF),
            pltpu.VMEM((blocks, GROUP, GROUP), F32),
            pltpu.VMEM((GROUP, 2 * pw), BF),
            pltpu.VMEM((tokens, LANES), F32),
            pltpu.VMEM((PARTS, nseq, 2 * rn, pw), F32),
            pltpu.VMEM((PARTS, nseq, 2 * rn, pw), F32),
            pltpu.VMEM((PARTS, nseq, 2 * rn, pw), F32),
            pltpu.VMEM((PARTS, nseq, 2 * rn, pw), F32),
            pltpu.VMEM((blocks, states, width), BF),
            pltpu.VMEM((blocks, states, width), BF),
            pltpu.VMEM((blocks, 8, width), F32),
            pltpu.VMEM((LANES, width), BF),
            pltpu.VMEM((LANES, width), BF),
            pltpu.VMEM((PARTS, 2 * pw, LANES), BF),
            pltpu.VMEM((8, width), F32),
            pltpu.VMEM((1, width), F32),
            pltpu.VMEM((8, LANES), F32),
            pltpu.VMEM((nseq, 8, LANES), F32),
            pltpu.VMEM((nseq, width), F32),
            pltpu.VMEM((nseq, 8, LANES), F32),
            pltpu.VMEM((nbatch, 8, LANES), F32),
            pltpu.VMEM((2, 8, LANES), F32),
            dma((2, blocks)),
            dma((PARTS, blocks)),
            dma((nseq,)),
            dma((nseq,)),
            dma((PARTS, nseq)),
            dma((PARTS, nseq)),
            dma((PARTS, nseq)),
            dma((PARTS, nseq)),
            dma((nseq,)),
            dma((nseq,)),
            dma((nbatch,)),
            dma((nbatch,)),
        ],
        compiler_params=pltpu.CompilerParams(
            collective_id=0, has_side_effects=True, vmem_limit_bytes=62 << 20
        ),
    )(inputs[0], cotangent[0], input_map[0], output_map[0], step_raw[0], par)
    return dx[None], db[None], dc[None], draw[None], gpar[0:2, 0:heads], gpar[2, 0:heads]


def solution(mesh):
    in_specs = (
        P("batch", "seq", None),
        P("batch", "seq", None),
        P("batch", "seq", None),
        P("batch", None, "seq"),
        P(),
        P(),
        P(),
        P("batch", "seq", None),
    )
    out_specs = (
        P("batch", "seq", None),
        P("batch", "seq", None),
        P("batch", "seq", None),
        P("batch", None, "seq"),
        P(),
        P(),
    )
    return jax.shard_map(shards, mesh=mesh, in_specs=in_specs, out_specs=out_specs, check_vma=False)
```

```python
import functools
import math

import jax
import jax.numpy as jnp
from jax import lax
from jax.experimental import pallas as pl
from jax.experimental.pallas import tpu as pltpu
from jax.sharding import PartitionSpec as P

GROUP = 256
LANES = 128
UNROLL = True
PARTS = (256, 512, 512, 512, 256)
MESH = pl.DeviceIdType.MESH
BF = jnp.bfloat16
F32 = jnp.float32


def dot(a, b):
    return jnp.dot(a, b, preferred_element_type=F32)


def dot_nt(a, b):
    return lax.dot_general(a, b, (((1,), (1,)), ((), ())), preferred_element_type=F32)


def two_parts(v):
    high = v.astype(BF).astype(F32)
    return high, v - high


def sum_dot(v, ones):
    high, rest = two_parts(v)
    mid, low = two_parts(rest)
    rows = v.shape[0]
    out = dot(jnp.concatenate([high, mid, low], axis=0).astype(BF), ones)
    return out[:rows] + out[rows : 2 * rows] + out[2 * rows :]


def kernel(
    nseq,
    nbatch,
    cuts,
    scale,
    x_hbm,
    dy_hbm,
    b_ref,
    c_ref,
    raw_ref,
    bias_ref,
    rate_ref,
    skip_ref,
    dx_hbm,
    db_ref,
    dc_ref,
    draw_ref,
    gpair_ref,
    grate_ref,
    x_buf,
    dy_buf,
    dyt_buf,
    fm_buf,
    dxp_buf,
    ds_buf,
    dg_buf,
    ecl_buf,
    step_buf,
    fac_buf,
    bt_buf,
    ct_buf,
    low_buf,
    up_buf,
    rc_buf,
    racc_buf,
    send_buf,
    recv_buf,
    back_buf,
    home_buf,
    stb_buf,
    gtb_buf,
    bdot_buf,
    ohp_buf,
    ohm_buf,
    ot_buf,
    skip_buf,
    skiprow_buf,
    dec_buf,
    decs_buf,
    decx_buf,
    p1_buf,
    p2_buf,
    mine_buf,
    in_sem,
    out_sem,
    s0,
    r0,
    s1,
    r1,
    s2,
    r2,
    s3,
    r3,
    s4,
    r4,
):
    tokens, width = x_buf.shape
    heads = raw_ref.shape[0]
    hs = width // heads
    states = b_ref.shape[1]
    blocks = tokens // GROUP
    parts = len(cuts)
    gw = 256
    starts = [sum(cuts[:q]) for q in range(parts)]

    def lanes_of(q):
        return slice(starts[q], starts[q] + cuts[q])

    rn = states // nseq
    chunk = max(rn, 16)
    me = lax.axis_index("seq")
    my_batch = lax.axis_index("batch")

    def rows_of(b):
        return pl.ds(pl.multiple_of(b * GROUP, GROUP), GROUP)

    def x_in(q):
        lanes = lanes_of(q)
        return pltpu.make_async_copy(x_hbm.at[:, lanes], x_buf.at[:, lanes], in_sem.at[0, q])

    def dy_in(q):
        lanes = lanes_of(q)
        return pltpu.make_async_copy(dy_hbm.at[:, lanes], dy_buf.at[:, lanes], in_sem.at[1, q])

    for q in range(parts):
        x_in(q).start()
        dy_in(q).start()

    bar = pltpu.get_barrier_semaphore()
    for k in range(1, nseq):
        pl.semaphore_signal(
            bar, inc=1, device_id={"seq": lax.rem(me + k, nseq)}, device_id_type=MESH
        )
    for k in range(1, nbatch):
        pl.semaphore_signal(
            bar, inc=1, device_id={"batch": lax.rem(my_batch + k, nbatch)}, device_id_type=MESH
        )

    k_id = lax.broadcasted_iota(jnp.int32, (LANES, width), 0)
    l_id = lax.broadcasted_iota(jnp.int32, (LANES, width), 1) // hs
    same = (k_id % heads) == l_id
    ohp_buf[...] = jnp.where(same & (k_id < 2 * heads), 1.0, 0.0).astype(BF)
    ohm_buf[...] = jnp.where(same & (k_id >= 2 * heads), 1.0, 0.0).astype(BF)

    eye = lax.broadcasted_iota(jnp.int32, (heads, LANES), 0) == lax.broadcasted_iota(
        jnp.int32, (heads, LANES), 1
    )
    head_lane = (
        lax.broadcasted_iota(jnp.int32, (heads, width), 0)
        == lax.broadcasted_iota(jnp.int32, (heads, width), 1) // hs
    )

    def column(row):
        return jnp.sum(jnp.where(eye[:, :heads], row, 0.0), axis=1, keepdims=True)

    def row(col):
        return jnp.sum(jnp.where(eye, col, 0.0), axis=0, keepdims=True)

    def expand(col):
        return jnp.sum(jnp.where(head_lane, col, 0.0), axis=0, keepdims=True)

    def per_head(line):
        return jnp.sum(jnp.where(head_lane, line, 0.0), axis=1, keepdims=True)

    bias = column(bias_ref[...])
    rate = column(rate_ref[...])
    skiprow_buf[...] = expand(column(skip_ref[...]))

    t_id = lax.broadcasted_iota(jnp.int32, (GROUP, GROUP), 0)
    s_id = lax.broadcasted_iota(jnp.int32, (GROUP, GROUP), 1)
    lower = s_id <= t_id
    upper = s_id >= t_id
    ones_le = jnp.where(upper, 1.0, 0.0).astype(BF)
    ones_ge = jnp.where(lower, 1.0, 0.0).astype(BF)

    skip_buf[...] = jnp.zeros_like(skip_buf)

    v_all = raw_ref[...] + bias
    step_all = jnp.maximum(v_all, 0.0) + jnp.log1p(jnp.exp(-jnp.abs(v_all)))
    log_all = -rate * step_all
    step_all = jnp.concatenate(
        [step_all[:, b * GROUP : (b + 1) * GROUP] for b in range(blocks)], axis=0
    )
    log_all = jnp.concatenate(
        [log_all[:, b * GROUP : (b + 1) * GROUP] for b in range(blocks)], axis=0
    )
    cum = sum_dot(log_all, ones_le)
    ep_all = jnp.exp(cum)
    em_all = step_all * jnp.exp(-cum)
    ep_hi, ep_lo = two_parts(ep_all)
    em_hi, em_lo = two_parts(em_all)
    total = jnp.ones((heads, 1), F32)
    for b in range(blocks):
        hb = slice(b * heads, (b + 1) * heads)
        step_buf[b] = step_all[hb]
        fac_buf[b] = jnp.concatenate(
            [ep_hi[hb], ep_lo[hb], em_hi[hb], em_lo[hb]], axis=0
        ).T.astype(BF)
        last = ep_all[hb, GROUP - 1 : GROUP]
        ecl_buf[b] = expand(last)
        total = total * last
        bt_buf[b] = b_ref[rows_of(b)].astype(F32).T.astype(BF)
        ct_buf[b] = c_ref[rows_of(b)].astype(F32).T.astype(BF)
    dec_buf[...] = jnp.broadcast_to(row(total), (8, LANES))

    def local(q):
        x_in(q).wait()
        dy_in(q).wait()

        def one_block(b, carry):
            rows = rows_of(b)
            fac = fac_buf[b]
            bt = bt_buf[b]
            ct = ct_buf[b]
            for g in range(cuts[q] // gw):
                lanes = slice(starts[q] + g * gw, starts[q] + (g + 1) * gw)
                fp = dot(fac, ohp_buf[:, lanes])
                fm = dot(fac, ohm_buf[:, lanes])
                fm_buf[rows, lanes] = fm
                xg = x_buf[rows, lanes].astype(F32)
                dyg = dy_buf[rows, lanes].astype(F32)
                xt = (xg * fm).astype(BF)
                dyt = (dyg * fp).astype(BF)
                x_buf[rows, lanes] = xt
                dyt_buf[rows, lanes] = dyt
                prod = xg * dyg
                skip_buf[:, lanes] += jnp.sum(prod.reshape(GROUP // 8, 8, gw), axis=0)
                ds_buf[b, :, lanes] = dot(bt, xt)
                dg_buf[b, :, lanes] = dot(ct, dyt)
            return carry

        lax.fori_loop(0, blocks, one_block, 0, unroll=UNROLL)
        lanes = lanes_of(q)
        for j in range(nseq):
            n = slice(j * rn, (j + 1) * rn)
            st = ds_buf[0, n, lanes] * ecl_buf[0, :, lanes]
            gt = dg_buf[0, n, lanes]
            decay = ecl_buf[0, :, lanes]
            for b in range(1, blocks):
                e = ecl_buf[b, :, lanes]
                st = (st + ds_buf[b, n, lanes]) * e
                gt = gt + decay * dg_buf[b, n, lanes]
                decay = decay * e
            send_buf[j, 0:rn, lanes] = st
            send_buf[j, rn:, lanes] = gt

    def decays(k):
        peer = lax.rem(me + k, nseq)
        return pltpu.make_async_remote_copy(
            src_ref=dec_buf,
            dst_ref=decs_buf.at[me],
            send_sem=s0.at[k],
            recv_sem=r0.at[k],
            device_id={"seq": peer},
            device_id_type=MESH,
        )

    def there(q, k):
        peer = lax.rem(me + k, nseq)
        return pltpu.make_async_remote_copy(
            src_ref=send_buf.at[peer, :, lanes_of(q)],
            dst_ref=recv_buf.at[me, :, lanes_of(q)],
            send_sem=s1.at[q, k],
            recv_sem=r1.at[q, k],
            device_id={"seq": peer},
            device_id_type=MESH,
        )

    def again(q, k):
        peer = lax.rem(me + k, nseq)
        return pltpu.make_async_remote_copy(
            src_ref=back_buf.at[peer, :, lanes_of(q)],
            dst_ref=home_buf.at[me, :, lanes_of(q)],
            send_sem=s2.at[q, k],
            recv_sem=r2.at[q, k],
            device_id={"seq": peer},
            device_id_type=MESH,
        )

    def scores(b, carry):
        bb = b_ref[rows_of(b)]
        cc = c_ref[rows_of(b)]
        low_buf[b] = jnp.where(lower, dot_nt(cc, bb), 0.0).astype(BF)
        up_buf[b] = jnp.where(upper, dot_nt(bb, cc), 0.0).astype(BF)
        return carry

    def inside(q):
        def one_block(b, carry):
            rows = rows_of(b)
            low = low_buf[b]
            up = up_buf[b]
            for g in range(cuts[q] // gw):
                lanes = slice(starts[q] + g * gw, starts[q] + (g + 1) * gw)
                xt = x_buf[rows, lanes]
                dyt = dyt_buf[rows, lanes]
                yi = dot(low, xt)
                dxi = dot(up, dyt)
                rc_buf[:, g * gw : (g + 1) * gw] = (yi * dyt.astype(F32)).astype(BF)
                rc_buf[:, cuts[q] + g * gw : cuts[q] + (g + 1) * gw] = (dxi * xt.astype(F32)).astype(BF)
                dxp_buf[rows, lanes] = fm_buf[rows, lanes] * dxi + skiprow_buf[
                    :, lanes
                ] * dy_buf[rows, lanes].astype(F32)
            red = dot(rc_buf[:, 0 : 2 * cuts[q]], ot_buf[2 * starts[q] : 2 * (starts[q] + cuts[q])])
            if q > 0:
                red = red + racc_buf[rows]
            racc_buf[rows] = red
            return carry

        lax.fori_loop(0, blocks, one_block, 0, unroll=UNROLL)

    def score_grads(b, carry):
        rows = rows_of(b)
        ds = jnp.where(lower, dot_nt(dyt_buf[rows], x_buf[rows]), 0.0)
        dc_ref[rows] = dot(ds.astype(BF), b_ref[rows])
        db_ref[rows] = dot(ds.T.astype(BF), c_ref[rows])
        return carry

    def scan(q):
        lanes = lanes_of(q)
        pw = cuts[q]
        for k in range(1, nseq):
            there(q, k).wait()
        st = jnp.zeros((rn, pw), F32)
        gt = jnp.zeros((rn, pw), F32)
        for i in range(nseq):
            back_buf[i, 0:rn, lanes] = st
            st = st * decx_buf[i : i + 1, lanes] + recv_buf[i, 0:rn, lanes]
            h = nseq - 1 - i
            back_buf[h, rn:, lanes] = gt
            gt = gt * decx_buf[h : h + 1, lanes] + recv_buf[h, rn:, lanes]
        for k in range(1, nseq):
            again(q, k).start()
        home_buf[me, :, lanes] = back_buf[me, :, lanes]

    def entering(q):
        lanes = lanes_of(q)
        pw = cuts[q]
        for k in range(1, nseq):
            again(q, k).wait()
        dots = [jnp.zeros((8, pw), F32) for _ in range(blocks)]
        for i in range(states // chunk):
            n = slice(i * chunk, (i + 1) * chunk)
            js = range(i * chunk // rn, (i + 1) * chunk // rn)
            st = jnp.concatenate([home_buf[j, 0:rn, lanes] for j in js], axis=0)
            ends = []
            for b in range(blocks):
                stb_buf[b, n, lanes] = st.astype(BF)
                st = (st + ds_buf[b, n, lanes]) * ecl_buf[b, :, lanes]
                ends.append(st)
            gt = jnp.concatenate([home_buf[j, rn:, lanes] for j in js], axis=0)
            for b in reversed(range(blocks)):
                prod = gt * ends[b]
                dots[b] = dots[b] + jnp.sum(prod.reshape(chunk // 8, 8, pw), axis=0)
                gt = gt * ecl_buf[b, :, lanes]
                gtb_buf[b, n, lanes] = gt.astype(BF)
                gt = gt + dg_buf[b, n, lanes]
        for b in range(blocks):
            bdot_buf[b, :, lanes] = dots[b]

    def dx_out(q, b):
        lanes = lanes_of(q)
        return pltpu.make_async_copy(
            dy_buf.at[rows_of(b), lanes], dx_hbm.at[rows_of(b), lanes], out_sem.at[q, b]
        )

    def finish(q):
        def one_block(b, carry):
            rows = rows_of(b)
            bb = b_ref[rows]
            cc = c_ref[rows]
            for g in range(cuts[q] // gw):
                lanes = slice(starts[q] + g * gw, starts[q] + (g + 1) * gw)
                yc = dot(cc, stb_buf[b, :, lanes])
                dxc = dot(bb, gtb_buf[b, :, lanes])
                rc_buf[:, g * gw : (g + 1) * gw] = (
                    yc * dyt_buf[rows, lanes].astype(F32)
                ).astype(BF)
                rc_buf[:, cuts[q] + g * gw : cuts[q] + (g + 1) * gw] = (
                    dxc * x_buf[rows, lanes].astype(F32)
                ).astype(BF)
                dx = fm_buf[rows, lanes] * dxc + dxp_buf[rows, lanes]
                dy_buf[rows, lanes] = dx.astype(BF)
            dx_out(q, b).start()
            red = racc_buf[rows] + dot(
                rc_buf[:, 0 : 2 * cuts[q]], ot_buf[2 * starts[q] : 2 * (starts[q] + cuts[q])]
            )
            if q < parts - 1:
                racc_buf[rows] = red
                return carry
            gbias, grate = carry
            dots = red.T
            rowdot = dots[0:heads]
            coldot = dots[heads : 2 * heads]
            ends = per_head(jnp.sum(bdot_buf[b], axis=0, keepdims=True))
            dlog = sum_dot(rowdot - coldot, ones_ge) + ends
            step = step_buf[b]
            v = raw_ref[:, rows] + bias
            draw = (coldot / step - rate * dlog) / (1.0 + jnp.exp(-v))
            draw_ref[:, rows] = draw
            gbias = gbias + jnp.sum(draw, axis=1, keepdims=True)
            grate = grate - jnp.sum(step * dlog, axis=1, keepdims=True)
            return gbias, grate

        zero = jnp.zeros((heads, 1), F32)
        return lax.fori_loop(0, blocks, one_block, (zero, zero), unroll=UNROLL)

    for q in range(parts):
        local(q)
        if q == 0:
            pl.semaphore_wait(bar, nseq + nbatch - 2)
        for k in range(1, nseq):
            there(q, k).start()
        if q == 0:
            for k in range(1, nseq):
                decays(k).start()
            decs_buf[me] = dec_buf[...]
        recv_buf[me, :, lanes_of(q)] = send_buf[me, :, lanes_of(q)]

    for q in range(parts):
        lanes = lanes_of(q)
        j_id = lax.broadcasted_iota(jnp.int32, (cuts[q], LANES), 1)
        h_id = (lax.broadcasted_iota(jnp.int32, (cuts[q], LANES), 0) + starts[q]) // hs
        ot_buf[2 * starts[q] : 2 * starts[q] + cuts[q]] = jnp.where(j_id == h_id, 1.0, 0.0).astype(
            BF
        )
        ot_buf[2 * starts[q] + cuts[q] : 2 * (starts[q] + cuts[q])] = jnp.where(
            j_id == h_id + heads, 1.0, 0.0
        ).astype(BF)
    lax.fori_loop(0, blocks, scores, 0, unroll=UNROLL)
    for q in range(parts):
        inside(q)
        if q == 0:
            for k in range(1, nseq):
                decays(k).wait()
            every = jnp.concatenate([decs_buf[i, 0:1] for i in range(nseq)], axis=0)
            high, rest = two_parts(every)
            mid, low = two_parts(rest)
            decx_buf[...] = (
                dot(high.astype(BF), ohp_buf[...])
                + dot(mid.astype(BF), ohp_buf[...])
                + dot(low.astype(BF), ohp_buf[...])
            )
        scan(q)
    lax.fori_loop(0, blocks, score_grads, 0)
    gskip = per_head(jnp.sum(skip_buf[...], axis=0, keepdims=True))

    for q in range(parts):
        entering(q)
        gbias, grate = finish(q)

    mine_buf[0] = jnp.concatenate(
        [row(gbias), row(gskip), row(grate), jnp.zeros((5, LANES), F32)], axis=0
    )

    def over_seq(k):
        peer = lax.rem(me + k, nseq)
        return pltpu.make_async_remote_copy(
            src_ref=mine_buf.at[0],
            dst_ref=p1_buf.at[me],
            send_sem=s3.at[k],
            recv_sem=r3.at[k],
            device_id={"seq": peer},
            device_id_type=MESH,
        )

    def over_batch(k):
        peer = lax.rem(my_batch + k, nbatch)
        return pltpu.make_async_remote_copy(
            src_ref=mine_buf.at[1],
            dst_ref=p2_buf.at[my_batch],
            send_sem=s4.at[k],
            recv_sem=r4.at[k],
            device_id={"batch": peer},
            device_id_type=MESH,
        )

    for k in range(1, nseq):
        over_seq(k).start()
    p1_buf[me] = mine_buf[0]

    def map_grads(b, carry):
        rows = rows_of(b)
        dc_ref[rows] += dot_nt(dyt_buf[rows], stb_buf[b])
        return carry

    lax.fori_loop(0, blocks, map_grads, 0)
    for k in range(1, nseq):
        over_seq(k).wait()
    total = p1_buf[0]
    for i in range(1, nseq):
        total = total + p1_buf[i]
    mine_buf[1] = total
    for k in range(1, nbatch):
        over_batch(k).start()
    p2_buf[my_batch] = total

    def other_grads(b, carry):
        rows = rows_of(b)
        db_ref[rows] += dot_nt(x_buf[rows], gtb_buf[b])
        return carry

    lax.fori_loop(0, blocks, other_grads, 0)
    for k in range(1, nbatch):
        over_batch(k).wait()
    total = p2_buf[0]
    for i in range(1, nbatch):
        total = total + p2_buf[i]
    total = total * scale
    gpair_ref[...] = total[0:2, 0:heads]
    grate_ref[...] = total[2:3, 0:heads]
    for b in range(blocks):
        for q in range(parts):
            dx_out(q, b).wait()


def shards(inputs, input_map, output_map, step_raw, step_bias, decay_rate, skip_gain, cotangent):
    tokens, width = inputs.shape[1:]
    heads = step_raw.shape[1]
    states = input_map.shape[2]
    nseq = lax.axis_size("seq")
    nbatch = lax.axis_size("batch")
    blocks = tokens // GROUP
    parts = len(PARTS)
    rn = states // nseq
    vmem = pl.BlockSpec(memory_space=pltpu.VMEM)
    hbm = pl.BlockSpec(memory_space=pl.ANY)
    dma = pltpu.SemaphoreType.DMA
    dx, db, dc, draw, gpair, grate = pl.pallas_call(
        functools.partial(kernel, nseq, nbatch, PARTS, 1.0 / math.sqrt(tokens * nseq * nbatch)),
        out_shape=(
            jax.ShapeDtypeStruct((tokens, width), BF),
            jax.ShapeDtypeStruct((tokens, states), F32),
            jax.ShapeDtypeStruct((tokens, states), F32),
            jax.ShapeDtypeStruct((heads, tokens), F32),
            jax.ShapeDtypeStruct((2, heads), F32),
            jax.ShapeDtypeStruct((1, heads), F32),
        ),
        in_specs=[hbm, hbm] + [vmem] * 6,
        out_specs=(hbm, vmem, vmem, vmem, vmem, vmem),
        scratch_shapes=[
            pltpu.VMEM((tokens, width), BF),
            pltpu.VMEM((tokens, width), BF),
            pltpu.VMEM((tokens, width), BF),
            pltpu.VMEM((tokens, width), F32),
            pltpu.VMEM((tokens, width), F32),
            pltpu.VMEM((blocks, states, width), F32),
            pltpu.VMEM((blocks, states, width), F32),
            pltpu.VMEM((blocks, 1, width), F32),
            pltpu.VMEM((blocks, heads, GROUP), F32),
            pltpu.VMEM((blocks, GROUP, LANES), BF),
            pltpu.VMEM((blocks, states, GROUP), BF),
            pltpu.VMEM((blocks, states, GROUP), BF),
            pltpu.VMEM((blocks, GROUP, GROUP), BF),
            pltpu.VMEM((blocks, GROUP, GROUP), BF),
            pltpu.VMEM((GROUP, 2 * max(PARTS)), BF),
            pltpu.VMEM((tokens, LANES), F32),
            pltpu.VMEM((nseq, 2 * rn, width), F32),
            pltpu.VMEM((nseq, 2 * rn, width), F32),
            pltpu.VMEM((nseq, 2 * rn, width), F32),
            pltpu.VMEM((nseq, 2 * rn, width), F32),
            pltpu.VMEM((blocks, states, width), BF),
            pltpu.VMEM((blocks, states, width), BF),
            pltpu.VMEM((blocks, 8, width), F32),
            pltpu.VMEM((LANES, width), BF),
            pltpu.VMEM((LANES, width), BF),
            pltpu.VMEM((2 * width, LANES), BF),
            pltpu.VMEM((8, width), F32),
            pltpu.VMEM((1, width), F32),
            pltpu.VMEM((8, LANES), F32),
            pltpu.VMEM((nseq, 8, LANES), F32),
            pltpu.VMEM((nseq, width), F32),
            pltpu.VMEM((nseq, 8, LANES), F32),
            pltpu.VMEM((nbatch, 8, LANES), F32),
            pltpu.VMEM((2, 8, LANES), F32),
            dma((2, parts)),
            dma((parts, blocks)),
            dma((nseq,)),
            dma((nseq,)),
            dma((parts, nseq)),
            dma((parts, nseq)),
            dma((parts, nseq)),
            dma((parts, nseq)),
            dma((nseq,)),
            dma((nseq,)),
            dma((nbatch,)),
            dma((nbatch,)),
        ],
        compiler_params=pltpu.CompilerParams(
            collective_id=0, has_side_effects=True, vmem_limit_bytes=62 << 20
        ),
    )(
        inputs[0],
        cotangent[0],
        input_map[0],
        output_map[0],
        step_raw[0],
        step_bias[None],
        decay_rate[None],
        skip_gain[None],
    )
    return dx[None], db[None], dc[None], draw[None], gpair, grate[0]


def solution(mesh):
    in_specs = (
        P("batch", "seq", None),
        P("batch", "seq", None),
        P("batch", "seq", None),
        P("batch", None, "seq"),
        P(),
        P(),
        P(),
        P("batch", "seq", None),
    )
    out_specs = (
        P("batch", "seq", None),
        P("batch", "seq", None),
        P("batch", "seq", None),
        P("batch", None, "seq"),
        P(),
        P(),
    )
    return jax.shard_map(shards, mesh=mesh, in_specs=in_specs, out_specs=out_specs, check_vma=False)
```

```python
import functools
import math

import jax
import jax.numpy as jnp
from jax import lax
from jax.experimental import pallas as pl
from jax.experimental.pallas import tpu as pltpu
from jax.sharding import PartitionSpec as P

GROUP = 256
LANES = 128
UNROLL = True
CHUNKS = (8, 1, 1, 1)
PARTS = (256, 512, 512, 512, 256)
MESH = pl.DeviceIdType.MESH
BF = jnp.bfloat16
F32 = jnp.float32


def dot(a, b):
    return jnp.dot(a, b, preferred_element_type=F32)


def dot_nt(a, b):
    return lax.dot_general(a, b, (((1,), (1,)), ((), ())), preferred_element_type=F32)


def two_parts(v):
    high = v.astype(BF).astype(F32)
    return high, v - high


def sum_dot(v, ones):
    high, rest = two_parts(v)
    mid, low = two_parts(rest)
    rows = v.shape[0]
    out = dot(jnp.concatenate([high, mid, low], axis=0).astype(BF), ones)
    return out[:rows] + out[rows : 2 * rows] + out[2 * rows :]


def kernel(
    nseq,
    nbatch,
    cuts,
    scale,
    x_hbm,
    dy_hbm,
    b_ref,
    c_ref,
    raw_ref,
    bias_ref,
    rate_ref,
    skip_ref,
    dx_hbm,
    db_ref,
    dc_ref,
    draw_ref,
    gpair_ref,
    grate_ref,
    x_buf,
    dy_buf,
    dyt_buf,
    fm_buf,
    dxp_buf,
    ds_buf,
    dg_buf,
    ecl_buf,
    step_buf,
    fac_buf,
    bt_buf,
    ct_buf,
    low_buf,
    up_buf,
    rc_buf,
    racc_buf,
    send_buf,
    recv_buf,
    back_buf,
    home_buf,
    stb_buf,
    gtb_buf,
    bdot_buf,
    ohp_buf,
    ohm_buf,
    ot_buf,
    skip_buf,
    skiprow_buf,
    dec_buf,
    decs_buf,
    decx_buf,
    p1_buf,
    p2_buf,
    mine_buf,
    in_sem,
    out_sem,
    s0,
    r0,
    s1,
    r1,
    s2,
    r2,
    s3,
    r3,
    s4,
    r4,
):
    tokens, width = x_buf.shape
    heads = raw_ref.shape[0]
    hs = width // heads
    states = b_ref.shape[1]
    blocks = tokens // GROUP
    parts = len(cuts)
    gw = 256
    starts = [sum(cuts[:q]) for q in range(parts)]

    def lanes_of(q):
        return slice(starts[q], starts[q] + cuts[q])

    rn = states // nseq
    chunk = max(rn, 16)
    me = lax.axis_index("seq")
    my_batch = lax.axis_index("batch")

    def rows_of(b):
        return pl.ds(pl.multiple_of(b * GROUP, GROUP), GROUP)

    def x_in(q):
        lanes = lanes_of(q)
        return pltpu.make_async_copy(x_hbm.at[:, lanes], x_buf.at[:, lanes], in_sem.at[0, q])

    def dy_in(q):
        lanes = lanes_of(q)
        return pltpu.make_async_copy(dy_hbm.at[:, lanes], dy_buf.at[:, lanes], in_sem.at[1, q])

    for q in range(parts):
        x_in(q).start()
        dy_in(q).start()

    bar = pltpu.get_barrier_semaphore()
    for k in range(1, nseq):
        pl.semaphore_signal(
            bar, inc=1, device_id={"seq": lax.rem(me + k, nseq)}, device_id_type=MESH
        )
    for k in range(1, nbatch):
        pl.semaphore_signal(
            bar, inc=1, device_id={"batch": lax.rem(my_batch + k, nbatch)}, device_id_type=MESH
        )

    k_id = lax.broadcasted_iota(jnp.int32, (LANES, width), 0)
    l_id = lax.broadcasted_iota(jnp.int32, (LANES, width), 1) // hs
    same = (k_id % heads) == l_id
    ohp_buf[...] = jnp.where(same & (k_id < 2 * heads), 1.0, 0.0).astype(BF)
    ohm_buf[...] = jnp.where(same & (k_id >= 2 * heads), 1.0, 0.0).astype(BF)

    eye = lax.broadcasted_iota(jnp.int32, (heads, LANES), 0) == lax.broadcasted_iota(
        jnp.int32, (heads, LANES), 1
    )
    head_lane = (
        lax.broadcasted_iota(jnp.int32, (heads, width), 0)
        == lax.broadcasted_iota(jnp.int32, (heads, width), 1) // hs
    )

    def column(row):
        return jnp.sum(jnp.where(eye[:, :heads], row, 0.0), axis=1, keepdims=True)

    def row(col):
        return jnp.sum(jnp.where(eye, col, 0.0), axis=0, keepdims=True)

    def expand(col):
        return jnp.sum(jnp.where(head_lane, col, 0.0), axis=0, keepdims=True)

    def per_head(line):
        return jnp.sum(jnp.where(head_lane, line, 0.0), axis=1, keepdims=True)

    bias = column(bias_ref[...])
    rate = column(rate_ref[...])
    skiprow_buf[...] = expand(column(skip_ref[...]))

    t_id = lax.broadcasted_iota(jnp.int32, (GROUP, GROUP), 0)
    s_id = lax.broadcasted_iota(jnp.int32, (GROUP, GROUP), 1)
    lower = s_id <= t_id
    upper = s_id >= t_id
    ones_le = jnp.where(upper, 1.0, 0.0).astype(BF)
    ones_ge = jnp.where(lower, 1.0, 0.0).astype(BF)

    skip_buf[...] = jnp.zeros_like(skip_buf)

    v_all = raw_ref[...] + bias
    step_all = jnp.maximum(v_all, 0.0) + jnp.log1p(jnp.exp(-jnp.abs(v_all)))
    log_all = -rate * step_all
    step_all = jnp.concatenate(
        [step_all[:, b * GROUP : (b + 1) * GROUP] for b in range(blocks)], axis=0
    )
    log_all = jnp.concatenate(
        [log_all[:, b * GROUP : (b + 1) * GROUP] for b in range(blocks)], axis=0
    )
    cum = sum_dot(log_all, ones_le)
    ep_all = jnp.exp(cum)
    em_all = step_all * jnp.exp(-cum)
    ep_hi, ep_lo = two_parts(ep_all)
    em_hi, em_lo = two_parts(em_all)
    total = jnp.ones((heads, 1), F32)
    for b in range(blocks):
        hb = slice(b * heads, (b + 1) * heads)
        step_buf[b] = step_all[hb]
        fac_buf[b] = jnp.concatenate(
            [ep_hi[hb], ep_lo[hb], em_hi[hb], em_lo[hb]], axis=0
        ).T.astype(BF)
        last = ep_all[hb, GROUP - 1 : GROUP]
        ecl_buf[b] = expand(last)
        total = total * last
        bt_buf[b] = b_ref[rows_of(b)].astype(F32).T.astype(BF)
        ct_buf[b] = c_ref[rows_of(b)].astype(F32).T.astype(BF)
    dec_buf[...] = jnp.broadcast_to(row(total), (8, LANES))

    def local(q):
        x_in(q).wait()
        dy_in(q).wait()

        def one_block(b, carry):
            rows = rows_of(b)
            fac = fac_buf[b]
            bt = bt_buf[b]
            ct = ct_buf[b]
            for g in range(cuts[q] // gw):
                lanes = slice(starts[q] + g * gw, starts[q] + (g + 1) * gw)
                fp = dot(fac, ohp_buf[:, lanes])
                fm = dot(fac, ohm_buf[:, lanes])
                fm_buf[rows, lanes] = fm
                xg = x_buf[rows, lanes].astype(F32)
                dyg = dy_buf[rows, lanes].astype(F32)
                xt = (xg * fm).astype(BF)
                dyt = (dyg * fp).astype(BF)
                x_buf[rows, lanes] = xt
                dyt_buf[rows, lanes] = dyt
                prod = xg * dyg
                skip_buf[:, lanes] += jnp.sum(prod.reshape(GROUP // 8, 8, gw), axis=0)
                ds_buf[b, :, lanes] = dot(bt, xt)
                dg_buf[b, :, lanes] = dot(ct, dyt)
            return carry

        lax.fori_loop(0, blocks, one_block, 0, unroll=UNROLL)
        lanes = lanes_of(q)
        for j in range(nseq):
            n = slice(j * rn, (j + 1) * rn)
            st = ds_buf[0, n, lanes] * ecl_buf[0, :, lanes]
            gt = dg_buf[0, n, lanes]
            decay = ecl_buf[0, :, lanes]
            for b in range(1, blocks):
                e = ecl_buf[b, :, lanes]
                st = (st + ds_buf[b, n, lanes]) * e
                gt = gt + decay * dg_buf[b, n, lanes]
                decay = decay * e
            send_buf[j, 0:rn, lanes] = st
            send_buf[j, rn:, lanes] = gt

    def decays(k):
        peer = lax.rem(me + k, nseq)
        return pltpu.make_async_remote_copy(
            src_ref=dec_buf,
            dst_ref=decs_buf.at[me],
            send_sem=s0.at[k],
            recv_sem=r0.at[k],
            device_id={"seq": peer},
            device_id_type=MESH,
        )

    def there(q, k):
        peer = lax.rem(me + k, nseq)
        return pltpu.make_async_remote_copy(
            src_ref=send_buf.at[peer, :, lanes_of(q)],
            dst_ref=recv_buf.at[me, :, lanes_of(q)],
            send_sem=s1.at[q, k],
            recv_sem=r1.at[q, k],
            device_id={"seq": peer},
            device_id_type=MESH,
        )

    def again(q, k):
        peer = lax.rem(me + k, nseq)
        return pltpu.make_async_remote_copy(
            src_ref=back_buf.at[peer, :, lanes_of(q)],
            dst_ref=home_buf.at[me, :, lanes_of(q)],
            send_sem=s2.at[q, k],
            recv_sem=r2.at[q, k],
            device_id={"seq": peer},
            device_id_type=MESH,
        )

    def scores(b, carry):
        bb = b_ref[rows_of(b)]
        cc = c_ref[rows_of(b)]
        low_buf[b] = jnp.where(lower, dot_nt(cc, bb), 0.0).astype(BF)
        up_buf[b] = jnp.where(upper, dot_nt(bb, cc), 0.0).astype(BF)
        return carry

    def inside(q):
        def one_block(b, carry):
            rows = rows_of(b)
            low = low_buf[b]
            up = up_buf[b]
            for g in range(cuts[q] // gw):
                lanes = slice(starts[q] + g * gw, starts[q] + (g + 1) * gw)
                xt = x_buf[rows, lanes]
                dyt = dyt_buf[rows, lanes]
                yi = dot(low, xt)
                dxi = dot(up, dyt)
                rc_buf[:, g * gw : (g + 1) * gw] = (yi * dyt.astype(F32)).astype(BF)
                rc_buf[:, cuts[q] + g * gw : cuts[q] + (g + 1) * gw] = (dxi * xt.astype(F32)).astype(BF)
                dxp_buf[rows, lanes] = fm_buf[rows, lanes] * dxi + skiprow_buf[
                    :, lanes
                ] * dy_buf[rows, lanes].astype(F32)
            red = dot(rc_buf[:, 0 : 2 * cuts[q]], ot_buf[2 * starts[q] : 2 * (starts[q] + cuts[q])])
            if q > 0:
                red = red + racc_buf[rows]
            racc_buf[rows] = red
            return carry

        lax.fori_loop(0, blocks, one_block, 0, unroll=UNROLL)

    def score_grads(b, carry):
        rows = rows_of(b)
        ds = jnp.where(lower, dot_nt(dyt_buf[rows], x_buf[rows]), 0.0)
        dc_ref[rows] = dot(ds.astype(BF), b_ref[rows])
        db_ref[rows] = dot(ds.T.astype(BF), c_ref[rows])
        return carry

    def scan(q):
        lanes = lanes_of(q)
        pw = cuts[q]
        for k in range(1, nseq):
            there(q, k).wait()
        st = jnp.zeros((rn, pw), F32)
        gt = jnp.zeros((rn, pw), F32)
        for i in range(nseq):
            back_buf[i, 0:rn, lanes] = st
            st = st * decx_buf[i : i + 1, lanes] + recv_buf[i, 0:rn, lanes]
            h = nseq - 1 - i
            back_buf[h, rn:, lanes] = gt
            gt = gt * decx_buf[h : h + 1, lanes] + recv_buf[h, rn:, lanes]
        for k in range(1, nseq):
            again(q, k).start()
        home_buf[me, :, lanes] = back_buf[me, :, lanes]

    def entering(q):
        lanes = lanes_of(q)
        pw = cuts[q]
        for k in range(1, nseq):
            again(q, k).wait()
        dots = [jnp.zeros((8, pw), F32) for _ in range(blocks)]
        for i in range(states // chunk):
            n = slice(i * chunk, (i + 1) * chunk)
            js = range(i * chunk // rn, (i + 1) * chunk // rn)
            st = jnp.concatenate([home_buf[j, 0:rn, lanes] for j in js], axis=0)
            ends = []
            for b in range(blocks):
                stb_buf[b, n, lanes] = st.astype(BF)
                st = (st + ds_buf[b, n, lanes]) * ecl_buf[b, :, lanes]
                ends.append(st)
            gt = jnp.concatenate([home_buf[j, rn:, lanes] for j in js], axis=0)
            for b in reversed(range(blocks)):
                prod = gt * ends[b]
                dots[b] = dots[b] + jnp.sum(prod.reshape(chunk // 8, 8, pw), axis=0)
                gt = gt * ecl_buf[b, :, lanes]
                gtb_buf[b, n, lanes] = gt.astype(BF)
                gt = gt + dg_buf[b, n, lanes]
        for b in range(blocks):
            bdot_buf[b, :, lanes] = dots[b]

    def dx_out(q, b):
        lanes = lanes_of(q)
        return pltpu.make_async_copy(
            dy_buf.at[rows_of(b), lanes], dx_hbm.at[rows_of(b), lanes], out_sem.at[q, b]
        )

    def finish(q):
        def one_block(b, carry):
            rows = rows_of(b)
            bb = b_ref[rows]
            cc = c_ref[rows]
            for g in range(cuts[q] // gw):
                lanes = slice(starts[q] + g * gw, starts[q] + (g + 1) * gw)
                yc = dot(cc, stb_buf[b, :, lanes])
                dxc = dot(bb, gtb_buf[b, :, lanes])
                rc_buf[:, g * gw : (g + 1) * gw] = (
                    yc * dyt_buf[rows, lanes].astype(F32)
                ).astype(BF)
                rc_buf[:, cuts[q] + g * gw : cuts[q] + (g + 1) * gw] = (
                    dxc * x_buf[rows, lanes].astype(F32)
                ).astype(BF)
                dx = fm_buf[rows, lanes] * dxc + dxp_buf[rows, lanes]
                dy_buf[rows, lanes] = dx.astype(BF)
            dx_out(q, b).start()
            red = racc_buf[rows] + dot(
                rc_buf[:, 0 : 2 * cuts[q]], ot_buf[2 * starts[q] : 2 * (starts[q] + cuts[q])]
            )
            if q < parts - 1:
                racc_buf[rows] = red
                return carry
            gbias, grate = carry
            dots = red.T
            rowdot = dots[0:heads]
            coldot = dots[heads : 2 * heads]
            ends = per_head(jnp.sum(bdot_buf[b], axis=0, keepdims=True))
            dlog = sum_dot(rowdot - coldot, ones_ge) + ends
            step = step_buf[b]
            v = raw_ref[:, rows] + bias
            draw = (coldot / step - rate * dlog) / (1.0 + jnp.exp(-v))
            draw_ref[:, rows] = draw
            gbias = gbias + jnp.sum(draw, axis=1, keepdims=True)
            grate = grate - jnp.sum(step * dlog, axis=1, keepdims=True)
            return gbias, grate

        zero = jnp.zeros((heads, 1), F32)
        return lax.fori_loop(0, blocks, one_block, (zero, zero), unroll=UNROLL)

    for q in range(parts):
        local(q)
        if q == 0:
            pl.semaphore_wait(bar, nseq + nbatch - 2)
        for k in range(1, nseq):
            there(q, k).start()
        if q == 0:
            for k in range(1, nseq):
                decays(k).start()
            decs_buf[me] = dec_buf[...]
        recv_buf[me, :, lanes_of(q)] = send_buf[me, :, lanes_of(q)]

    for q in range(parts):
        lanes = lanes_of(q)
        j_id = lax.broadcasted_iota(jnp.int32, (cuts[q], LANES), 1)
        h_id = (lax.broadcasted_iota(jnp.int32, (cuts[q], LANES), 0) + starts[q]) // hs
        ot_buf[2 * starts[q] : 2 * starts[q] + cuts[q]] = jnp.where(j_id == h_id, 1.0, 0.0).astype(
            BF
        )
        ot_buf[2 * starts[q] + cuts[q] : 2 * (starts[q] + cuts[q])] = jnp.where(
            j_id == h_id + heads, 1.0, 0.0
        ).astype(BF)
    lax.fori_loop(0, blocks, scores, 0, unroll=UNROLL)
    for q in range(parts):
        inside(q)
        if q == 0:
            for k in range(1, nseq):
                decays(k).wait()
            every = jnp.concatenate([decs_buf[i, 0:1] for i in range(nseq)], axis=0)
            high, rest = two_parts(every)
            mid, low = two_parts(rest)
            decx_buf[...] = (
                dot(high.astype(BF), ohp_buf[...])
                + dot(mid.astype(BF), ohp_buf[...])
                + dot(low.astype(BF), ohp_buf[...])
            )
        scan(q)
    lax.fori_loop(0, blocks, score_grads, 0)
    gskip = per_head(jnp.sum(skip_buf[...], axis=0, keepdims=True))

    for q in range(parts):
        entering(q)
        gbias, grate = finish(q)

    mine_buf[0] = jnp.concatenate(
        [row(gbias), row(gskip), row(grate), jnp.zeros((5, LANES), F32)], axis=0
    )

    def over_seq(k):
        peer = lax.rem(me + k, nseq)
        return pltpu.make_async_remote_copy(
            src_ref=mine_buf.at[0],
            dst_ref=p1_buf.at[me],
            send_sem=s3.at[k],
            recv_sem=r3.at[k],
            device_id={"seq": peer},
            device_id_type=MESH,
        )

    def over_batch(k):
        peer = lax.rem(my_batch + k, nbatch)
        return pltpu.make_async_remote_copy(
            src_ref=mine_buf.at[1],
            dst_ref=p2_buf.at[my_batch],
            send_sem=s4.at[k],
            recv_sem=r4.at[k],
            device_id={"batch": peer},
            device_id_type=MESH,
        )

    for k in range(1, nseq):
        over_seq(k).start()
    p1_buf[me] = mine_buf[0]

    def map_grads(b, carry):
        rows = rows_of(b)
        dc_ref[rows] += dot_nt(dyt_buf[rows], stb_buf[b])
        return carry

    lax.fori_loop(0, blocks, map_grads, 0)
    for k in range(1, nseq):
        over_seq(k).wait()
    total = p1_buf[0]
    for i in range(1, nseq):
        total = total + p1_buf[i]
    mine_buf[1] = total
    for k in range(1, nbatch):
        over_batch(k).start()
    p2_buf[my_batch] = total

    def other_grads(b, carry):
        rows = rows_of(b)
        db_ref[rows] += dot_nt(x_buf[rows], gtb_buf[b])
        return carry

    lax.fori_loop(0, blocks, other_grads, 0)
    for k in range(1, nbatch):
        over_batch(k).wait()
    total = p2_buf[0]
    for i in range(1, nbatch):
        total = total + p2_buf[i]
    total = total * scale
    gpair_ref[...] = total[0:2, 0:heads]
    grate_ref[...] = total[2:3, 0:heads]
    for b in range(blocks):
        for q in range(parts):
            dx_out(q, b).wait()


def deliver(chunks, *refs):
    count = len(chunks)
    buffers = refs[2 * count : 3 * count]
    sems = refs[3 * count]
    pairs = []
    for i in range(count):
        rows = buffers[i].shape[0] // chunks[i]
        for c in range(chunks[i]):
            part = pl.ds(c * rows, rows)
            k = len(pairs)
            pairs.append(
                (
                    pltpu.make_async_copy(refs[i].at[part], buffers[i].at[part], sems.at[0, k]),
                    pltpu.make_async_copy(
                        buffers[i].at[part], refs[count + i].at[part], sems.at[1, k]
                    ),
                )
            )
    for load, _ in pairs:
        load.start()
    for load, store in pairs:
        load.wait()
        store.start()
    for _, store in pairs:
        store.wait()


def shards(inputs, input_map, output_map, step_raw, step_bias, decay_rate, skip_gain, cotangent):
    tokens, width = inputs.shape[1:]
    heads = step_raw.shape[1]
    states = input_map.shape[2]
    nseq = lax.axis_size("seq")
    nbatch = lax.axis_size("batch")
    blocks = tokens // GROUP
    parts = len(PARTS)
    rn = states // nseq
    vmem = pl.BlockSpec(memory_space=pltpu.VMEM)
    hbm = pl.BlockSpec(memory_space=pl.ANY)
    dma = pltpu.SemaphoreType.DMA
    dx, db, dc, draw, gpair, grate = pl.pallas_call(
        functools.partial(kernel, nseq, nbatch, PARTS, 1.0 / math.sqrt(tokens * nseq * nbatch)),
        out_shape=(
            jax.ShapeDtypeStruct((tokens, width), BF),
            jax.ShapeDtypeStruct((tokens, states), F32),
            jax.ShapeDtypeStruct((tokens, states), F32),
            jax.ShapeDtypeStruct((heads, tokens), F32),
            jax.ShapeDtypeStruct((2, heads), F32),
            jax.ShapeDtypeStruct((1, heads), F32),
        ),
        in_specs=[hbm, hbm] + [vmem] * 6,
        out_specs=(hbm, vmem, vmem, vmem, vmem, vmem),
        scratch_shapes=[
            pltpu.VMEM((tokens, width), BF),
            pltpu.VMEM((tokens, width), BF),
            pltpu.VMEM((tokens, width), BF),
            pltpu.VMEM((tokens, width), F32),
            pltpu.VMEM((tokens, width), F32),
            pltpu.VMEM((blocks, states, width), F32),
            pltpu.VMEM((blocks, states, width), F32),
            pltpu.VMEM((blocks, 1, width), F32),
            pltpu.VMEM((blocks, heads, GROUP), F32),
            pltpu.VMEM((blocks, GROUP, LANES), BF),
            pltpu.VMEM((blocks, states, GROUP), BF),
            pltpu.VMEM((blocks, states, GROUP), BF),
            pltpu.VMEM((blocks, GROUP, GROUP), BF),
            pltpu.VMEM((blocks, GROUP, GROUP), BF),
            pltpu.VMEM((GROUP, 2 * max(PARTS)), BF),
            pltpu.VMEM((tokens, LANES), F32),
            pltpu.VMEM((nseq, 2 * rn, width), F32),
            pltpu.VMEM((nseq, 2 * rn, width), F32),
            pltpu.VMEM((nseq, 2 * rn, width), F32),
            pltpu.VMEM((nseq, 2 * rn, width), F32),
            pltpu.VMEM((blocks, states, width), BF),
            pltpu.VMEM((blocks, states, width), BF),
            pltpu.VMEM((blocks, 8, width), F32),
            pltpu.VMEM((LANES, width), BF),
            pltpu.VMEM((LANES, width), BF),
            pltpu.VMEM((2 * width, LANES), BF),
            pltpu.VMEM((8, width), F32),
            pltpu.VMEM((1, width), F32),
            pltpu.VMEM((8, LANES), F32),
            pltpu.VMEM((nseq, 8, LANES), F32),
            pltpu.VMEM((nseq, width), F32),
            pltpu.VMEM((nseq, 8, LANES), F32),
            pltpu.VMEM((nbatch, 8, LANES), F32),
            pltpu.VMEM((2, 8, LANES), F32),
            dma((2, parts)),
            dma((parts, blocks)),
            dma((nseq,)),
            dma((nseq,)),
            dma((parts, nseq)),
            dma((parts, nseq)),
            dma((parts, nseq)),
            dma((parts, nseq)),
            dma((nseq,)),
            dma((nseq,)),
            dma((nbatch,)),
            dma((nbatch,)),
        ],
        compiler_params=pltpu.CompilerParams(
            collective_id=0, has_side_effects=True, vmem_limit_bytes=62 << 20
        ),
    )(
        inputs[0],
        cotangent[0],
        input_map[0],
        output_map[0],
        step_raw[0],
        step_bias[None],
        decay_rate[None],
        skip_gain[None],
    )
    arrays = (dx, db, dc, draw)
    chunks = CHUNKS
    dx, db, dc, draw = pl.pallas_call(
        functools.partial(deliver, chunks),
        out_shape=tuple(jax.ShapeDtypeStruct(a.shape, a.dtype) for a in arrays),
        in_specs=[hbm] * len(arrays),
        out_specs=(hbm,) * len(arrays),
        scratch_shapes=[pltpu.VMEM(a.shape, a.dtype) for a in arrays] + [dma((2, sum(chunks)))],
        compiler_params=pltpu.CompilerParams(vmem_limit_bytes=62 << 20),
    )(*arrays)
    return dx[None], db[None], dc[None], draw[None], gpair, grate[0]


def solution(mesh):
    in_specs = (
        P("batch", "seq", None),
        P("batch", "seq", None),
        P("batch", "seq", None),
        P("batch", None, "seq"),
        P(),
        P(),
        P(),
        P("batch", "seq", None),
    )
    out_specs = (
        P("batch", "seq", None),
        P("batch", "seq", None),
        P("batch", "seq", None),
        P("batch", None, "seq"),
        P(),
        P(),
    )
    return jax.shard_map(shards, mesh=mesh, in_specs=in_specs, out_specs=out_specs, check_vma=False)
```

```python
import functools
import math

import jax
import jax.numpy as jnp
from jax import lax
from jax.experimental import pallas as pl
from jax.experimental.pallas import tpu as pltpu
from jax.sharding import PartitionSpec as P

GROUP = 256
LANES = 128
UNROLL = True
CHUNKS = (8, 1, 1, 1)
PARTS = (256, 512, 512, 512, 256)
MESH = pl.DeviceIdType.MESH
BF = jnp.bfloat16
F32 = jnp.float32


def dot(a, b):
    return jnp.dot(a, b, preferred_element_type=F32)


def dot_nt(a, b):
    return lax.dot_general(a, b, (((1,), (1,)), ((), ())), preferred_element_type=F32)


def two_parts(v):
    high = v.astype(BF).astype(F32)
    return high, v - high


def sum_dot(v, ones):
    high, rest = two_parts(v)
    mid, low = two_parts(rest)
    rows = v.shape[0]
    out = dot(jnp.concatenate([high, mid, low], axis=0).astype(BF), ones)
    return out[:rows] + out[rows : 2 * rows] + out[2 * rows :]


def kernel(
    nseq,
    nbatch,
    cuts,
    scale,
    x_hbm,
    dy_hbm,
    b_hbm,
    c_hbm,
    raw_hbm,
    bias_ref,
    rate_ref,
    skip_ref,
    dx_hbm,
    db_ref,
    dc_ref,
    draw_ref,
    gpair_ref,
    grate_ref,
    x_buf,
    dy_buf,
    dyt_buf,
    fm_buf,
    dxp_buf,
    ds_buf,
    dg_buf,
    ecl_buf,
    step_buf,
    fac_buf,
    bt_buf,
    ct_buf,
    low_buf,
    up_buf,
    rc_buf,
    racc_buf,
    send_buf,
    recv_buf,
    back_buf,
    home_buf,
    stb_buf,
    gtb_buf,
    bdot_buf,
    ohp_buf,
    ohm_buf,
    ot_buf,
    skip_buf,
    skiprow_buf,
    dec_buf,
    decs_buf,
    decx_buf,
    p1_buf,
    p2_buf,
    mine_buf,
    b_ref,
    c_ref,
    raw_ref,
    map_sem,
    in_sem,
    out_sem,
    s0,
    r0,
    s1,
    r1,
    s2,
    r2,
    s3,
    r3,
    s4,
    r4,
):
    tokens, width = x_buf.shape
    heads = raw_ref.shape[0]
    hs = width // heads
    states = b_ref.shape[1]
    blocks = tokens // GROUP
    parts = len(cuts)
    gw = 256
    starts = [sum(cuts[:q]) for q in range(parts)]

    def lanes_of(q):
        return slice(starts[q], starts[q] + cuts[q])

    rn = states // nseq
    chunk = max(rn, 16)
    me = lax.axis_index("seq")
    my_batch = lax.axis_index("batch")

    def rows_of(b):
        return pl.ds(pl.multiple_of(b * GROUP, GROUP), GROUP)

    def x_in(q):
        lanes = lanes_of(q)
        return pltpu.make_async_copy(x_hbm.at[:, lanes], x_buf.at[:, lanes], in_sem.at[0, q])

    def dy_in(q):
        lanes = lanes_of(q)
        return pltpu.make_async_copy(dy_hbm.at[:, lanes], dy_buf.at[:, lanes], in_sem.at[1, q])

    raw_in = pltpu.make_async_copy(raw_hbm, raw_ref, map_sem.at[0])
    b_in = pltpu.make_async_copy(b_hbm, b_ref, map_sem.at[1])
    c_in = pltpu.make_async_copy(c_hbm, c_ref, map_sem.at[2])
    raw_in.start()
    b_in.start()
    c_in.start()
    for q in range(parts):
        x_in(q).start()
        dy_in(q).start()

    bar = pltpu.get_barrier_semaphore()
    for k in range(1, nseq):
        pl.semaphore_signal(
            bar, inc=1, device_id={"seq": lax.rem(me + k, nseq)}, device_id_type=MESH
        )
    for k in range(1, nbatch):
        pl.semaphore_signal(
            bar, inc=1, device_id={"batch": lax.rem(my_batch + k, nbatch)}, device_id_type=MESH
        )

    k_id = lax.broadcasted_iota(jnp.int32, (LANES, width), 0)
    l_id = lax.broadcasted_iota(jnp.int32, (LANES, width), 1) // hs
    same = (k_id % heads) == l_id
    ohp_buf[...] = jnp.where(same & (k_id < 2 * heads), 1.0, 0.0).astype(BF)
    ohm_buf[...] = jnp.where(same & (k_id >= 2 * heads), 1.0, 0.0).astype(BF)

    eye = lax.broadcasted_iota(jnp.int32, (heads, LANES), 0) == lax.broadcasted_iota(
        jnp.int32, (heads, LANES), 1
    )
    head_lane = (
        lax.broadcasted_iota(jnp.int32, (heads, width), 0)
        == lax.broadcasted_iota(jnp.int32, (heads, width), 1) // hs
    )

    def column(row):
        return jnp.sum(jnp.where(eye[:, :heads], row, 0.0), axis=1, keepdims=True)

    def row(col):
        return jnp.sum(jnp.where(eye, col, 0.0), axis=0, keepdims=True)

    def expand(col):
        return jnp.sum(jnp.where(head_lane, col, 0.0), axis=0, keepdims=True)

    def per_head(line):
        return jnp.sum(jnp.where(head_lane, line, 0.0), axis=1, keepdims=True)

    bias = column(bias_ref[...])
    rate = column(rate_ref[...])
    skiprow_buf[...] = expand(column(skip_ref[...]))

    t_id = lax.broadcasted_iota(jnp.int32, (GROUP, GROUP), 0)
    s_id = lax.broadcasted_iota(jnp.int32, (GROUP, GROUP), 1)
    lower = s_id <= t_id
    upper = s_id >= t_id
    ones_le = jnp.where(upper, 1.0, 0.0).astype(BF)
    ones_ge = jnp.where(lower, 1.0, 0.0).astype(BF)

    skip_buf[...] = jnp.zeros_like(skip_buf)

    raw_in.wait()
    v_all = raw_ref[...] + bias
    step_all = jnp.maximum(v_all, 0.0) + jnp.log1p(jnp.exp(-jnp.abs(v_all)))
    log_all = -rate * step_all
    step_all = jnp.concatenate(
        [step_all[:, b * GROUP : (b + 1) * GROUP] for b in range(blocks)], axis=0
    )
    log_all = jnp.concatenate(
        [log_all[:, b * GROUP : (b + 1) * GROUP] for b in range(blocks)], axis=0
    )
    cum = sum_dot(log_all, ones_le)
    ep_all = jnp.exp(cum)
    em_all = step_all * jnp.exp(-cum)
    ep_hi, ep_lo = two_parts(ep_all)
    em_hi, em_lo = two_parts(em_all)
    b_in.wait()
    c_in.wait()
    total = jnp.ones((heads, 1), F32)
    for b in range(blocks):
        hb = slice(b * heads, (b + 1) * heads)
        step_buf[b] = step_all[hb]
        fac_buf[b] = jnp.concatenate(
            [ep_hi[hb], ep_lo[hb], em_hi[hb], em_lo[hb]], axis=0
        ).T.astype(BF)
        last = ep_all[hb, GROUP - 1 : GROUP]
        ecl_buf[b] = expand(last)
        total = total * last
        bt_buf[b] = b_ref[rows_of(b)].astype(F32).T.astype(BF)
        ct_buf[b] = c_ref[rows_of(b)].astype(F32).T.astype(BF)
    dec_buf[...] = jnp.broadcast_to(row(total), (8, LANES))

    def local(q):
        x_in(q).wait()
        dy_in(q).wait()

        def one_block(b, carry):
            rows = rows_of(b)
            fac = fac_buf[b]
            bt = bt_buf[b]
            ct = ct_buf[b]
            for g in range(cuts[q] // gw):
                lanes = slice(starts[q] + g * gw, starts[q] + (g + 1) * gw)
                fp = dot(fac, ohp_buf[:, lanes])
                fm = dot(fac, ohm_buf[:, lanes])
                fm_buf[rows, lanes] = fm
                xg = x_buf[rows, lanes].astype(F32)
                dyg = dy_buf[rows, lanes].astype(F32)
                xt = (xg * fm).astype(BF)
                dyt = (dyg * fp).astype(BF)
                x_buf[rows, lanes] = xt
                dyt_buf[rows, lanes] = dyt
                prod = xg * dyg
                skip_buf[:, lanes] += jnp.sum(prod.reshape(GROUP // 8, 8, gw), axis=0)
                ds_buf[b, :, lanes] = dot(bt, xt)
                dg_buf[b, :, lanes] = dot(ct, dyt)
            return carry

        lax.fori_loop(0, blocks, one_block, 0, unroll=UNROLL)
        lanes = lanes_of(q)
        for j in range(nseq):
            n = slice(j * rn, (j + 1) * rn)
            st = ds_buf[0, n, lanes] * ecl_buf[0, :, lanes]
            gt = dg_buf[0, n, lanes]
            decay = ecl_buf[0, :, lanes]
            for b in range(1, blocks):
                e = ecl_buf[b, :, lanes]
                st = (st + ds_buf[b, n, lanes]) * e
                gt = gt + decay * dg_buf[b, n, lanes]
                decay = decay * e
            send_buf[j, 0:rn, lanes] = st
            send_buf[j, rn:, lanes] = gt

    def decays(k):
        peer = lax.rem(me + k, nseq)
        return pltpu.make_async_remote_copy(
            src_ref=dec_buf,
            dst_ref=decs_buf.at[me],
            send_sem=s0.at[k],
            recv_sem=r0.at[k],
            device_id={"seq": peer},
            device_id_type=MESH,
        )

    def there(q, k):
        peer = lax.rem(me + k, nseq)
        return pltpu.make_async_remote_copy(
            src_ref=send_buf.at[peer, :, lanes_of(q)],
            dst_ref=recv_buf.at[me, :, lanes_of(q)],
            send_sem=s1.at[q, k],
            recv_sem=r1.at[q, k],
            device_id={"seq": peer},
            device_id_type=MESH,
        )

    def again(q, k):
        peer = lax.rem(me + k, nseq)
        return pltpu.make_async_remote_copy(
            src_ref=back_buf.at[peer, :, lanes_of(q)],
            dst_ref=home_buf.at[me, :, lanes_of(q)],
            send_sem=s2.at[q, k],
            recv_sem=r2.at[q, k],
            device_id={"seq": peer},
            device_id_type=MESH,
        )

    def scores(b, carry):
        bb = b_ref[rows_of(b)]
        cc = c_ref[rows_of(b)]
        low_buf[b] = jnp.where(lower, dot_nt(cc, bb), 0.0).astype(BF)
        up_buf[b] = jnp.where(upper, dot_nt(bb, cc), 0.0).astype(BF)
        return carry

    def inside(q):
        def one_block(b, carry):
            rows = rows_of(b)
            low = low_buf[b]
            up = up_buf[b]
            for g in range(cuts[q] // gw):
                lanes = slice(starts[q] + g * gw, starts[q] + (g + 1) * gw)
                xt = x_buf[rows, lanes]
                dyt = dyt_buf[rows, lanes]
                yi = dot(low, xt)
                dxi = dot(up, dyt)
                rc_buf[:, g * gw : (g + 1) * gw] = (yi * dyt.astype(F32)).astype(BF)
                rc_buf[:, cuts[q] + g * gw : cuts[q] + (g + 1) * gw] = (dxi * xt.astype(F32)).astype(BF)
                dxp_buf[rows, lanes] = fm_buf[rows, lanes] * dxi + skiprow_buf[
                    :, lanes
                ] * dy_buf[rows, lanes].astype(F32)
            red = dot(rc_buf[:, 0 : 2 * cuts[q]], ot_buf[2 * starts[q] : 2 * (starts[q] + cuts[q])])
            if q > 0:
                red = red + racc_buf[rows]
            racc_buf[rows] = red
            return carry

        lax.fori_loop(0, blocks, one_block, 0, unroll=UNROLL)

    def score_grads(b, carry):
        rows = rows_of(b)
        ds = jnp.where(lower, dot_nt(dyt_buf[rows], x_buf[rows]), 0.0)
        dc_ref[rows] = dot(ds.astype(BF), b_ref[rows])
        db_ref[rows] = dot(ds.T.astype(BF), c_ref[rows])
        return carry

    def scan(q):
        lanes = lanes_of(q)
        pw = cuts[q]
        for k in range(1, nseq):
            there(q, k).wait()
        st = jnp.zeros((rn, pw), F32)
        gt = jnp.zeros((rn, pw), F32)
        for i in range(nseq):
            back_buf[i, 0:rn, lanes] = st
            st = st * decx_buf[i : i + 1, lanes] + recv_buf[i, 0:rn, lanes]
            h = nseq - 1 - i
            back_buf[h, rn:, lanes] = gt
            gt = gt * decx_buf[h : h + 1, lanes] + recv_buf[h, rn:, lanes]
        for k in range(1, nseq):
            again(q, k).start()
        home_buf[me, :, lanes] = back_buf[me, :, lanes]

    def entering(q):
        lanes = lanes_of(q)
        pw = cuts[q]
        for k in range(1, nseq):
            again(q, k).wait()
        dots = [jnp.zeros((8, pw), F32) for _ in range(blocks)]
        for i in range(states // chunk):
            n = slice(i * chunk, (i + 1) * chunk)
            js = range(i * chunk // rn, (i + 1) * chunk // rn)
            st = jnp.concatenate([home_buf[j, 0:rn, lanes] for j in js], axis=0)
            ends = []
            for b in range(blocks):
                stb_buf[b, n, lanes] = st.astype(BF)
                st = (st + ds_buf[b, n, lanes]) * ecl_buf[b, :, lanes]
                ends.append(st)
            gt = jnp.concatenate([home_buf[j, rn:, lanes] for j in js], axis=0)
            for b in reversed(range(blocks)):
                prod = gt * ends[b]
                dots[b] = dots[b] + jnp.sum(prod.reshape(chunk // 8, 8, pw), axis=0)
                gt = gt * ecl_buf[b, :, lanes]
                gtb_buf[b, n, lanes] = gt.astype(BF)
                gt = gt + dg_buf[b, n, lanes]
        for b in range(blocks):
            bdot_buf[b, :, lanes] = dots[b]

    def dx_out(q, b):
        lanes = lanes_of(q)
        return pltpu.make_async_copy(
            dy_buf.at[rows_of(b), lanes], dx_hbm.at[rows_of(b), lanes], out_sem.at[q, b]
        )

    def finish(q):
        def one_block(b, carry):
            rows = rows_of(b)
            bb = b_ref[rows]
            cc = c_ref[rows]
            for g in range(cuts[q] // gw):
                lanes = slice(starts[q] + g * gw, starts[q] + (g + 1) * gw)
                yc = dot(cc, stb_buf[b, :, lanes])
                dxc = dot(bb, gtb_buf[b, :, lanes])
                rc_buf[:, g * gw : (g + 1) * gw] = (
                    yc * dyt_buf[rows, lanes].astype(F32)
                ).astype(BF)
                rc_buf[:, cuts[q] + g * gw : cuts[q] + (g + 1) * gw] = (
                    dxc * x_buf[rows, lanes].astype(F32)
                ).astype(BF)
                dx = fm_buf[rows, lanes] * dxc + dxp_buf[rows, lanes]
                dy_buf[rows, lanes] = dx.astype(BF)
            dx_out(q, b).start()
            red = racc_buf[rows] + dot(
                rc_buf[:, 0 : 2 * cuts[q]], ot_buf[2 * starts[q] : 2 * (starts[q] + cuts[q])]
            )
            if q < parts - 1:
                racc_buf[rows] = red
                return carry
            gbias, grate = carry
            dots = red.T
            rowdot = dots[0:heads]
            coldot = dots[heads : 2 * heads]
            ends = per_head(jnp.sum(bdot_buf[b], axis=0, keepdims=True))
            dlog = sum_dot(rowdot - coldot, ones_ge) + ends
            step = step_buf[b]
            v = raw_ref[:, rows] + bias
            draw = (coldot / step - rate * dlog) / (1.0 + jnp.exp(-v))
            draw_ref[:, rows] = draw
            gbias = gbias + jnp.sum(draw, axis=1, keepdims=True)
            grate = grate - jnp.sum(step * dlog, axis=1, keepdims=True)
            return gbias, grate

        zero = jnp.zeros((heads, 1), F32)
        return lax.fori_loop(0, blocks, one_block, (zero, zero), unroll=UNROLL)

    for q in range(parts):
        local(q)
        if q == 0:
            pl.semaphore_wait(bar, nseq + nbatch - 2)
        for k in range(1, nseq):
            there(q, k).start()
        if q == 0:
            for k in range(1, nseq):
                decays(k).start()
            decs_buf[me] = dec_buf[...]
        recv_buf[me, :, lanes_of(q)] = send_buf[me, :, lanes_of(q)]

    for q in range(parts):
        lanes = lanes_of(q)
        j_id = lax.broadcasted_iota(jnp.int32, (cuts[q], LANES), 1)
        h_id = (lax.broadcasted_iota(jnp.int32, (cuts[q], LANES), 0) + starts[q]) // hs
        ot_buf[2 * starts[q] : 2 * starts[q] + cuts[q]] = jnp.where(j_id == h_id, 1.0, 0.0).astype(
            BF
        )
        ot_buf[2 * starts[q] + cuts[q] : 2 * (starts[q] + cuts[q])] = jnp.where(
            j_id == h_id + heads, 1.0, 0.0
        ).astype(BF)
    lax.fori_loop(0, blocks, scores, 0, unroll=UNROLL)
    for q in range(parts):
        inside(q)
        if q == 0:
            for k in range(1, nseq):
                decays(k).wait()
            every = jnp.concatenate([decs_buf[i, 0:1] for i in range(nseq)], axis=0)
            high, rest = two_parts(every)
            mid, low = two_parts(rest)
            decx_buf[...] = (
                dot(high.astype(BF), ohp_buf[...])
                + dot(mid.astype(BF), ohp_buf[...])
                + dot(low.astype(BF), ohp_buf[...])
            )
        scan(q)
    lax.fori_loop(0, blocks, score_grads, 0)
    gskip = per_head(jnp.sum(skip_buf[...], axis=0, keepdims=True))

    for q in range(parts):
        entering(q)
        gbias, grate = finish(q)

    mine_buf[0] = jnp.concatenate(
        [row(gbias), row(gskip), row(grate), jnp.zeros((5, LANES), F32)], axis=0
    )

    def over_seq(k):
        peer = lax.rem(me + k, nseq)
        return pltpu.make_async_remote_copy(
            src_ref=mine_buf.at[0],
            dst_ref=p1_buf.at[me],
            send_sem=s3.at[k],
            recv_sem=r3.at[k],
            device_id={"seq": peer},
            device_id_type=MESH,
        )

    def over_batch(k):
        peer = lax.rem(my_batch + k, nbatch)
        return pltpu.make_async_remote_copy(
            src_ref=mine_buf.at[1],
            dst_ref=p2_buf.at[my_batch],
            send_sem=s4.at[k],
            recv_sem=r4.at[k],
            device_id={"batch": peer},
            device_id_type=MESH,
        )

    for k in range(1, nseq):
        over_seq(k).start()
    p1_buf[me] = mine_buf[0]

    def map_grads(b, carry):
        rows = rows_of(b)
        dc_ref[rows] += dot_nt(dyt_buf[rows], stb_buf[b])
        return carry

    lax.fori_loop(0, blocks, map_grads, 0)
    for k in range(1, nseq):
        over_seq(k).wait()
    total = p1_buf[0]
    for i in range(1, nseq):
        total = total + p1_buf[i]
    mine_buf[1] = total
    for k in range(1, nbatch):
        over_batch(k).start()
    p2_buf[my_batch] = total

    def other_grads(b, carry):
        rows = rows_of(b)
        db_ref[rows] += dot_nt(x_buf[rows], gtb_buf[b])
        return carry

    lax.fori_loop(0, blocks, other_grads, 0)
    for k in range(1, nbatch):
        over_batch(k).wait()
    total = p2_buf[0]
    for i in range(1, nbatch):
        total = total + p2_buf[i]
    total = total * scale
    gpair_ref[...] = total[0:2, 0:heads]
    grate_ref[...] = total[2:3, 0:heads]
    for b in range(blocks):
        for q in range(parts):
            dx_out(q, b).wait()


def deliver(chunks, *refs):
    count = len(chunks)
    buffers = refs[2 * count : 3 * count]
    sems = refs[3 * count]
    pairs = []
    for i in range(count):
        rows = buffers[i].shape[0] // chunks[i]
        for c in range(chunks[i]):
            part = pl.ds(c * rows, rows)
            k = len(pairs)
            pairs.append(
                (
                    pltpu.make_async_copy(refs[i].at[part], buffers[i].at[part], sems.at[0, k]),
                    pltpu.make_async_copy(
                        buffers[i].at[part], refs[count + i].at[part], sems.at[1, k]
                    ),
                )
            )
    for load, _ in pairs:
        load.start()
    for load, store in pairs:
        load.wait()
        store.start()
    for _, store in pairs:
        store.wait()


def shards(inputs, input_map, output_map, step_raw, step_bias, decay_rate, skip_gain, cotangent):
    tokens, width = inputs.shape[1:]
    heads = step_raw.shape[1]
    states = input_map.shape[2]
    nseq = lax.axis_size("seq")
    nbatch = lax.axis_size("batch")
    blocks = tokens // GROUP
    parts = len(PARTS)
    rn = states // nseq
    vmem = pl.BlockSpec(memory_space=pltpu.VMEM)
    hbm = pl.BlockSpec(memory_space=pl.ANY)
    dma = pltpu.SemaphoreType.DMA
    dx, db, dc, draw, gpair, grate = pl.pallas_call(
        functools.partial(kernel, nseq, nbatch, PARTS, 1.0 / math.sqrt(tokens * nseq * nbatch)),
        out_shape=(
            jax.ShapeDtypeStruct((tokens, width), BF),
            jax.ShapeDtypeStruct((tokens, states), F32),
            jax.ShapeDtypeStruct((tokens, states), F32),
            jax.ShapeDtypeStruct((heads, tokens), F32),
            jax.ShapeDtypeStruct((2, heads), F32),
            jax.ShapeDtypeStruct((1, heads), F32),
        ),
        in_specs=[hbm] * 5 + [vmem] * 3,
        out_specs=(hbm, vmem, vmem, vmem, vmem, vmem),
        scratch_shapes=[
            pltpu.VMEM((tokens, width), BF),
            pltpu.VMEM((tokens, width), BF),
            pltpu.VMEM((tokens, width), BF),
            pltpu.VMEM((tokens, width), F32),
            pltpu.VMEM((tokens, width), F32),
            pltpu.VMEM((blocks, states, width), F32),
            pltpu.VMEM((blocks, states, width), F32),
            pltpu.VMEM((blocks, 1, width), F32),
            pltpu.VMEM((blocks, heads, GROUP), F32),
            pltpu.VMEM((blocks, GROUP, LANES), BF),
            pltpu.VMEM((blocks, states, GROUP), BF),
            pltpu.VMEM((blocks, states, GROUP), BF),
            pltpu.VMEM((blocks, GROUP, GROUP), BF),
            pltpu.VMEM((blocks, GROUP, GROUP), BF),
            pltpu.VMEM((GROUP, 2 * max(PARTS)), BF),
            pltpu.VMEM((tokens, LANES), F32),
            pltpu.VMEM((nseq, 2 * rn, width), F32),
            pltpu.VMEM((nseq, 2 * rn, width), F32),
            pltpu.VMEM((nseq, 2 * rn, width), F32),
            pltpu.VMEM((nseq, 2 * rn, width), F32),
            pltpu.VMEM((blocks, states, width), BF),
            pltpu.VMEM((blocks, states, width), BF),
            pltpu.VMEM((blocks, 8, width), F32),
            pltpu.VMEM((LANES, width), BF),
            pltpu.VMEM((LANES, width), BF),
            pltpu.VMEM((2 * width, LANES), BF),
            pltpu.VMEM((8, width), F32),
            pltpu.VMEM((1, width), F32),
            pltpu.VMEM((8, LANES), F32),
            pltpu.VMEM((nseq, 8, LANES), F32),
            pltpu.VMEM((nseq, width), F32),
            pltpu.VMEM((nseq, 8, LANES), F32),
            pltpu.VMEM((nbatch, 8, LANES), F32),
            pltpu.VMEM((2, 8, LANES), F32),
            pltpu.VMEM((tokens, states), BF),
            pltpu.VMEM((tokens, states), BF),
            pltpu.VMEM((heads, tokens), F32),
            dma((3,)),
            dma((2, parts)),
            dma((parts, blocks)),
            dma((nseq,)),
            dma((nseq,)),
            dma((parts, nseq)),
            dma((parts, nseq)),
            dma((parts, nseq)),
            dma((parts, nseq)),
            dma((nseq,)),
            dma((nseq,)),
            dma((nbatch,)),
            dma((nbatch,)),
        ],
        compiler_params=pltpu.CompilerParams(
            collective_id=0, has_side_effects=True, vmem_limit_bytes=62 << 20
        ),
    )(
        inputs[0],
        cotangent[0],
        input_map[0],
        output_map[0],
        step_raw[0],
        step_bias[None],
        decay_rate[None],
        skip_gain[None],
    )
    arrays = (dx, db, dc, draw)
    chunks = CHUNKS
    dx, db, dc, draw = pl.pallas_call(
        functools.partial(deliver, chunks),
        out_shape=tuple(jax.ShapeDtypeStruct(a.shape, a.dtype) for a in arrays),
        in_specs=[hbm] * len(arrays),
        out_specs=(hbm,) * len(arrays),
        scratch_shapes=[pltpu.VMEM(a.shape, a.dtype) for a in arrays] + [dma((2, sum(chunks)))],
        compiler_params=pltpu.CompilerParams(vmem_limit_bytes=62 << 20),
    )(*arrays)
    return dx[None], db[None], dc[None], draw[None], gpair, grate[0]


def solution(mesh):
    in_specs = (
        P("batch", "seq", None),
        P("batch", "seq", None),
        P("batch", "seq", None),
        P("batch", None, "seq"),
        P(),
        P(),
        P(),
        P("batch", "seq", None),
    )
    out_specs = (
        P("batch", "seq", None),
        P("batch", "seq", None),
        P("batch", "seq", None),
        P("batch", None, "seq"),
        P(),
        P(),
    )
    return jax.shard_map(shards, mesh=mesh, in_specs=in_specs, out_specs=out_specs, check_vma=False)
```
